256 devices in a mesh: leaf: 32 (over x, z), rows: 8 (over y, core).
Axes of the slice: x: 4, y: 4, z: 8, core: 2. Of those that a mesh axis runs over, the one named last changes fastest.
Arguments:
- child_front_entries: float32 [32, 2, 8, 128, 2048], P('leaf', None, 'rows'), may hold values from 0 to 2, as said below
- parent_fronts: float32 [32, 2, 8, 128, 2048], P('leaf', None, 'rows'), may hold values from 0 to 2, as said below
- parent_of: int32 [32], replicated, may hold values from 0 to 15, never falling along the last dimension, each value on 1 to 4 neighbouring positions
- positions: int32 [32, 8], P('leaf'), may hold values from 0 to 15, as said below
Outputs:
- child_factor: float32 [32, 2, 8, 128, 1024], P('leaf', None, 'rows')
- parent_factor: float32 [32, 2, 8, 128, 1024], P('leaf', None, 'rows')
- parent_contribution_block: float32 [32, 1, 8, 128, 1024], P('leaf', None, 'rows')
The draws below stay inside these ranges and needn't reach their ends.
Inputs may be any that keep to these rules, and one draw needn't show every extreme that they name: `parent_of`: children of one parent stand at consecutive indices, at most 4 of them, and some parent has exactly 4; every parent has a child. `positions`: each row lists 8 distinct parent block numbers in increasing order; the last is always 16 - 1. `child_front_entries`: each front is symmetric positive definite. `parent_fronts`: each front is symmetric positive definite.
All inputs are finite; a program needn't handle non-finite values.
Results may differ from the reference program's by a relative error of at most 0.000078.
Values sent between devices are 32-bit elements; how exact they have to be, the bound alone decides.
No kernel may reach another device: no remote copies, remote signals or barrier semaphores. Data moves between devices by JAX's collectives and lax.ppermute only.
A program may use at most 256 MiB of HBM per device.

```python
import math
import jax
import jax.numpy as jnp
import numpy as np
from jax import lax

F = 2048
B = 128
PIV = 1024
MOST = 4
CHILDREN = 32
PARENTS = 16
FB = 16
CBW = 1024
CB_BLK = 8
N_ROWS = 8


def kernel_front(sub_key):
    sub_keys = jax.random.split(sub_key, 3)
    box_side = 2.6
    centers = jax.random.uniform(sub_keys[0], (FB, 1, 3), jnp.float32, 0.0, box_side)
    jitter = jax.random.uniform(sub_keys[1], (FB, B, 3), jnp.float32, -0.3, 0.3)
    points = (centers + jitter).reshape(F, 3)
    diagonal_jitter_term = jax.random.uniform(sub_keys[2], (F,), jnp.float32, 0.3, 1.0)
    squared = jnp.zeros((F, F), jnp.float32)
    for coord_no in range(3):
        coord_gap = points[:, coord_no][:, None] - points[:, coord_no][None, :]
        squared = squared + coord_gap * coord_gap
    distance = jnp.sqrt(squared)
    closeness = jnp.maximum(1.0 - distance, 0.0)
    kernel_value = closeness ** 4 * (4.0 * distance + 1.0)
    return kernel_value + jnp.diag(diagonal_jitter_term)


def front_scales(base_key):
    phase = jax.random.uniform(jax.random.fold_in(base_key, 53), (), jnp.float32, 0.0, 6.2831853)
    front_index = jnp.arange(CHILDREN, dtype=jnp.float32)
    weight_level = 0.5 + 0.5 * jnp.sin(phase + 0.15 * front_index)
    return jnp.exp(-4.0 * 2.302585093 * weight_level)


def draw_fronts(front_key, base_key):
    sub_keys = jax.random.split(front_key, CHILDREN)
    fronts = lax.map(kernel_front, sub_keys)
    scales = front_scales(base_key)
    fronts = fronts * scales[:, None, None]
    return fronts.reshape(CHILDREN, FB // N_ROWS, N_ROWS, B, F)


def draw_child_front_entries(key, part):
    return draw_fronts(jax.random.fold_in(key, 11), key)


def draw_parent_fronts(key, part):
    return draw_fronts(jax.random.fold_in(key, 23), key)


def draw_positions(key, part):
    scores = jax.random.randint(jax.random.fold_in(key, 37), (CHILDREN, FB - 1), 0, 1 << 20) * FB + jnp.arange(FB - 1, dtype=jnp.int32)
    top_scores = lax.top_k(scores, CB_BLK - 1)[1]
    chosen = jnp.sort(top_scores.astype(jnp.int32), axis=-1)
    last_block = jnp.full((CHILDREN, 1), FB - 1, jnp.int32)
    return jnp.concatenate([chosen, last_block], axis=1)


def profile(amount, total, most, lean):
    loads = [(1 << 20) // math.isqrt(standing ** lean) + 1 for standing in range(2, amount + 1)]
    rest, holding = total - most - (amount - 1), [1] * (amount - 1)
    while rest > 0:
        candidates = [i for i in range(amount - 1) if holding[i] < most]
        whole, budget = sum([loads[i] for i in candidates]), rest
        for i in candidates:
            more = min(most - holding[i], max(1, budget * loads[i] // whole), rest)
            holding[i] = holding[i] + more
            rest = rest - more
    return np.array([most] + holding)


def ragged_sizes(own_key, number_of, total, bound, lean):
    if number_of == 2:
        one = jax.random.randint(own_key, (), max(1, total - bound), min(bound, total - 1) + 1)
        return jnp.stack([one, total - one])
    lengths = jnp.asarray(profile(number_of, total, bound, lean), jnp.int32)
    pairs = (number_of - 1) // 2
    giver, sink = lengths[1:1 + 2 * pairs:2], lengths[2:2 + 2 * pairs:2]
    room = jnp.minimum(giver - 1, bound - sink)
    shifted = jax.random.randint(jax.random.fold_in(own_key, 1), (pairs,), 0, 1 << 20) % (room + 1)
    lengths = lengths.at[1:1 + 2 * pairs:2].set(giver - shifted).at[2:2 + 2 * pairs:2].set(sink + shifted)
    return lengths[jax.random.permutation(jax.random.fold_in(own_key, 2), number_of)]


def setup_inputs(seed: int = 0) -> dict:
    arg_keys = jax.random.split(jax.random.key(seed), 5)
    child_front_entries = draw_child_front_entries(jax.random.fold_in(arg_keys[4], 71), 0)
    parent_fronts = draw_parent_fronts(jax.random.fold_in(arg_keys[4], 71), 0)
    parent_of = jnp.searchsorted(jnp.cumsum(ragged_sizes(arg_keys[2], PARENTS, CHILDREN, MOST, 2)), jnp.arange(CHILDREN), side="right").astype(jnp.int32)
    positions = draw_positions(jax.random.fold_in(arg_keys[4], 71), 0)
    return {"child_front_entries": child_front_entries, "parent_fronts": parent_fronts, "parent_of": parent_of, "positions": positions}


def factor_front(front_matrix):
    pivot_part = front_matrix[:PIV, :PIV]
    lower_factor = jnp.linalg.cholesky(pivot_part)
    below_factor = lax.linalg.triangular_solve(lower_factor, front_matrix[PIV:, :PIV], left_side=False, lower=True, transpose_a=True)
    factor_cols = jnp.concatenate([lower_factor, below_factor], axis=0)
    schur_part = front_matrix[PIV:, PIV:] - jnp.dot(below_factor, below_factor.T, precision=lax.Precision.HIGHEST)
    return (factor_cols, schur_part)

def reference(child_front_entries, parent_fronts, parent_of, positions):
    child_total = child_front_entries.shape[0]
    child_mats = child_front_entries.reshape(child_total, F, F)
    parent_mats = parent_fronts.reshape(child_total, F, F)
    child_cols, child_updates = lax.map(factor_front, child_mats)
    block_onehot = (positions[:, :, None] == jnp.arange(FB, dtype=jnp.int32)[None, None, :]).astype(jnp.float32)
    update_blocks = child_updates.reshape(child_total, CB_BLK, B, CB_BLK, B)
    extended = jnp.einsum('kap,kaibj,kbq->kpiqj', block_onehot, update_blocks, block_onehot, precision=lax.Precision.HIGHEST)
    extended = extended.reshape(child_total, F, F)
    previous = jnp.concatenate([jnp.full((1,), -1, jnp.int32), parent_of[:-1]])
    head_flags = parent_of != previous
    leaf_ids = jnp.arange(child_total, dtype=jnp.int32)
    head_of = lax.cummax(jnp.where(head_flags, leaf_ids, 0), axis=0).astype(jnp.int32)
    assembled = parent_mats.at[head_of].add(extended)
    parent_cols, parent_schur = lax.map(factor_front, assembled)
    head_mask = head_flags.astype(jnp.float32)[:, None, None]
    parent_cols = parent_cols * head_mask
    parent_schur = parent_schur * head_mask
    child_out = child_cols.reshape(child_total, FB // N_ROWS, N_ROWS, B, PIV)
    parent_out = parent_cols.reshape(child_total, FB // N_ROWS, N_ROWS, B, PIV)
    update_out = parent_schur.reshape(child_total, CB_BLK // N_ROWS, N_ROWS, B, CBW)
    return (child_out, parent_out, update_out)
```

```python
import jax
import jax.numpy as jnp
from jax import lax
from jax.experimental import pallas as pl
from jax.experimental.pallas import tpu as pltpu
from jax.sharding import PartitionSpec as P

B = 128
PIV = 1024
NB = PIV // B
MIB = 2**20
DN = (((1,), (1,)), ((), ()))

def split(x):
    hi = x.astype(jnp.bfloat16)
    lo = (x - hi.astype(jnp.float32)).astype(jnp.bfloat16)
    return hi, lo

def dot(a, b):
    return lax.dot_general(a, b, DN, preferred_element_type=jnp.float32)

def mm(a, b):
    (ah, al), (bh, bl) = a, b
    return dot(ah, bh) + (dot(ah, bl) + dot(al, bh))

def wide(x):
    return jnp.broadcast_to(x, (8, B))

def diag_factor(a_ref, e_ref, u_ref, v_ref):
    sub = lax.broadcasted_iota(jnp.int32, (8, B), 0)
    rows = lax.broadcasted_iota(jnp.int32, (B, B), 0)
    cols = lax.broadcasted_iota(jnp.int32, (B, B), 1)
    e_ref[...] = jnp.where(rows == cols, 1.0, 0.0)

    def panel(p, _):
        v = a_ref[0:8, :]
        er = e_ref[0:8, :]
        c = [wide(v[:, j:j + 1]) for j in range(8)]
        s = [[wide(c[j][i:i + 1, :]) if i >= j else None for j in range(8)] for i in range(8)]
        rolled = pltpu.roll(v, B - 8, 1)
        vr = [wide(rolled[j:j + 1, :]) for j in range(8)]
        ev = [wide(er[j:j + 1, :]) for j in range(8)]
        r = [None] * 8
        for j in range(8):
            r[j] = lax.rsqrt(s[j][j])
            for i in range(j + 1, 8):
                s[i][j] = s[i][j] * r[j]
            for k in range(j + 1, 8):
                for i in range(k, 8):
                    s[i][k] = s[i][k] - s[i][j] * s[k][j]
            vr[j] = vr[j] * r[j]
            ev[j] = ev[j] * r[j]
            for i in range(j + 1, 8):
                vr[i] = vr[i] - s[i][j] * vr[j]
                ev[i] = ev[i] - s[i][j] * ev[j]
        urows, erows = vr[0], ev[0]
        for j in range(1, 8):
            urows = jnp.where(sub == j, vr[j], urows)
            erows = jnp.where(sub == j, ev[j], erows)
        at = pl.multiple_of(p * 8, 8)
        u_ref[pl.ds(at, 8), :] = pltpu.roll(urows, p * 8 + 8, 1)
        v_ref[pl.ds(at, 8), :] = erows
        w, we = list(vr), list(ev)
        for j in range(7, -1, -1):
            w[j] = w[j] * r[j]
            we[j] = we[j] * r[j]
            for k in range(j):
                w[k] = w[k] - s[j][k] * w[j]
                we[k] = we[k] - s[j][k] * we[j]
        for q in range(1, 16):
            aq = a_ref[8 * q:8 * q + 8, :]
            eq = e_ref[8 * q:8 * q + 8, :]
            cq = [wide(aq[:, j:j + 1]) for j in range(8)]
            ar = pltpu.roll(aq, B - 8, 1)
            for j in range(8):
                ar = ar - cq[j] * w[j]
                eq = eq - cq[j] * we[j]
            a_ref[8 * q - 8:8 * q, :] = ar
            e_ref[8 * q - 8:8 * q, :] = eq
        return 0

    lax.fori_loop(0, 16, panel, 0)
    u_ref[...] = jnp.where(cols >= rows, u_ref[...], 0.0)

def chol_kernel(g_ref, l_ref, dinv_ref, s_ref, hi_ref, lo_ref, a_ref, e_ref, u_ref, v_ref):
    for k in range(NB):
        k0, k1 = k * B, k * B + B
        if k == 0:
            for i in range(NB):
                s_ref[i * B:i * B + B, :] = g_ref[i, :, :]
                l_ref[i * B:i * B + B, :] = jnp.zeros((B, NB * B), jnp.float32)
        a_ref[...] = s_ref[k0:k1, k0:k1]
        diag_factor(a_ref, e_ref, u_ref, v_ref)
        l_ref[k0:k1, k0:k1] = u_ref[...].T
        inv = v_ref[...]
        dinv_ref[k] = inv
        if k + 1 < NB:
            n = NB * B - k1
            x = mm(split(s_ref[k1:, k0:k1]), split(inv))
            l_ref[k1:, k0:k1] = x
            h, l = split(x)
            hi_ref[k1:, :] = h
            lo_ref[k1:, :] = l
            for j in range(k + 1, NB):
                j0 = j * B
                s_ref[j0:, j0:j0 + B] = s_ref[j0:, j0:j0 + B] - mm(
                    (hi_ref[j0:, :], lo_ref[j0:, :]), (hi_ref[j0:j0 + B, :], lo_ref[j0:j0 + B, :]))

def chol(g):
    return pl.pallas_call(
        chol_kernel,
        out_shape=(
            jax.ShapeDtypeStruct((PIV, PIV), jnp.float32),
            jax.ShapeDtypeStruct((NB, B, B), jnp.float32),
        ),
        scratch_shapes=[
            pltpu.VMEM((PIV, PIV), jnp.float32),
            pltpu.VMEM((PIV, B), jnp.bfloat16),
            pltpu.VMEM((PIV, B), jnp.bfloat16),
        ]
        + [pltpu.VMEM((B, B), jnp.float32)] * 4,
        compiler_params=pltpu.CompilerParams(vmem_limit_bytes=40 * MIB),
        cost_estimate=pl.CostEstimate(flops=60 * 10**9, bytes_accessed=8 * MIB, transcendentals=0),
        name="chol",
    )(g)


def solve_below(l_ref, dinv_ref, rp_ref, xh_ref, xl_ref):
    for k in range(NB):
        k0, k1 = k * B, k * B + B
        c = rp_ref[:, :, k0:k1].reshape(PIV, B)
        if k > 0:
            c = c - mm((xh_ref[:, :k0], xl_ref[:, :k0]), split(l_ref[k0:k1, :k0]))
        h, l = split(mm(split(c), split(dinv_ref[k])))
        xh_ref[:, k0:k1] = h
        xl_ref[:, k0:k1] = l


def rows_at(ref, block):
    return ref[pl.ds(pl.multiple_of(block * B, B), B), :]


def child_kernel(meta_ref, l_ref, dinv_ref, rp_ref, rr_ref, fac_ref, ep_ref, er_ref, xh_ref, xl_ref):
    solve_below(l_ref, dinv_ref, rp_ref, xh_ref, xl_ref)
    me = meta_ref[0]
    fac_ref[0] = rows_at(l_ref, me)
    fac_ref[1] = rows_at(xh_ref, me).astype(jnp.float32) + rows_at(xl_ref, me).astype(jnp.float32)
    x = (xh_ref[...], xl_ref[...])
    for half, out_ref in ((0, ep_ref), (1, er_ref)):
        a = jnp.int32(-1)
        for b in range(NB):
            a = jnp.where(meta_ref[1 + b] == me + half * NB, b, a)
        held = a >= 0
        a = jnp.maximum(a, 0)
        u = rr_ref[a] - mm((rows_at(xh_ref, a), rows_at(xl_ref, a)), x)
        u = jnp.where(held, u, 0.0)
        out_ref[...] = jnp.zeros_like(out_ref)
        for b in range(NB):
            at = meta_ref[1 + b]
            if half == 0:
                @pl.when(at < NB)
                def _():
                    out_ref[:, pl.ds(pl.multiple_of(at * B, B), B)] = u[:, b * B:b * B + B]
            else:
                out_ref[:, pl.ds(pl.multiple_of(at * B, B), B)] = u[:, b * B:b * B + B]


def parent_kernel(meta_ref, l_ref, dinv_ref, rp_ref, rr_ref, fac_ref, cb_ref, xh_ref, xl_ref):
    solve_below(l_ref, dinv_ref, rp_ref, xh_ref, xl_ref)
    me = meta_ref[0]
    keep = meta_ref[9] > 0
    fac_ref[0] = jnp.where(keep, rows_at(l_ref, me), 0.0)
    xh, xl = rows_at(xh_ref, me), rows_at(xl_ref, me)
    fac_ref[1] = jnp.where(keep, xh.astype(jnp.float32) + xl.astype(jnp.float32), 0.0)
    u = rr_ref[...] - mm((xh, xl), (xh_ref[...], xl_ref[...]))
    cb_ref[...] = jnp.where(keep, u, 0.0)


def tail(kernel, name, outs, *args):
    return pl.pallas_call(
        kernel,
        in_specs=[pl.BlockSpec(memory_space=pltpu.SMEM)] + [pl.BlockSpec(memory_space=pltpu.VMEM)] * 4,
        out_shape=tuple(jax.ShapeDtypeStruct(s, jnp.float32) for s in outs),
        scratch_shapes=[pltpu.VMEM((PIV, PIV), jnp.bfloat16)] * 2,
        compiler_params=pltpu.CompilerParams(vmem_limit_bytes=40 * MIB),
        cost_estimate=pl.CostEstimate(flops=10 * 10**9, bytes_accessed=16 * MIB, transcendentals=0),
        name=name,
    )(*args)


def from_right(x, shift, same):
    leaves = lax.axis_size("leaf")
    got = lax.ppermute(x, "leaf", [(i + shift, i) for i in range(leaves - shift)])
    return x + jnp.where(same, got, 0.0)


def on_device(child_front_entries, parent_fronts, parent_of, positions):
    me = lax.axis_index("rows")
    leaf = lax.axis_index("leaf")
    child = child_front_entries[0, :, 0]
    parent = parent_fronts[0, :, 0]

    leaves = lax.axis_size("leaf")
    padded = jnp.concatenate([jnp.full((1,), -1, jnp.int32), parent_of, jnp.full((2,), -1, jnp.int32)])
    near = lax.dynamic_slice(padded, (leaf,), (4,))
    head = near[1] != near[0]
    same1, same2 = near[1] == near[2], near[1] == near[3]
    meta = jnp.concatenate(
        [me.astype(jnp.int32)[None], positions[0], head.astype(jnp.int32)[None]]
    )

    pp = lax.all_gather(child[0, :, :PIV], "rows")
    rp = lax.all_gather(child[1, :, :PIV], "rows")
    rr = lax.all_gather(child[1, :, PIV:], "rows")
    l, dinv = chol(pp)
    child_out, ext_p, ext_r = tail(
        child_kernel, "child_tail", ((2, B, PIV), (B, PIV), (B, 2 * PIV)), meta, l, dinv, rp, rr
    )
    sum_p = from_right(from_right(ext_p, 1, same1), 2, same2)
    sum_r = from_right(from_right(ext_r, 1, same1), 2, same2)
    pp = lax.all_gather(parent[0, :, :PIV] + sum_p, "rows")
    low = parent[1] + sum_r
    rp = lax.all_gather(low[:, :PIV], "rows")
    l, dinv = chol(pp)
    parent_out, block_out = tail(
        parent_kernel, "parent_tail", ((2, B, PIV), (B, PIV)), meta, l, dinv, rp, low[:, PIV:]
    )
    return (
        child_out[None, :, None],
        parent_out[None, :, None],
        block_out[None, None, None],
    )


def solution(mesh):
    placed = P("leaf", None, "rows", None, None)
    return jax.shard_map(
        on_device,
        mesh=mesh,
        in_specs=(placed, placed, P(), P("leaf", None)),
        out_specs=(placed, placed, placed),
        check_vma=False,
    )
```

```python
import functools

import jax
import jax.numpy as jnp
from jax import lax
from jax.experimental import pallas as pl
from jax.experimental.pallas import tpu as pltpu
from jax.sharding import PartitionSpec as P


B = 128
PIV = 1024
NB = PIV // B
NY = NB // 2
SLOTS = 5
CUT = 4
KW = 16
STEP = 8
MIB = 2**20
DN = (((1,), (1,)), ((), ()))


def split(x):
    hi = x.astype(jnp.bfloat16)
    lo = (x - hi.astype(jnp.float32)).astype(jnp.bfloat16)
    return hi, lo


def dot(a, b):
    return lax.dot_general(a, b, DN, preferred_element_type=jnp.float32)


def mm(a, b):
    (ah, al), (bh, bl) = a, b
    return dot(ah, bh) + (dot(ah, bl) + dot(al, bh))


def wide(x):
    return jnp.broadcast_to(x, (8, B))


def pick(x, i):
    return jnp.take_along_axis(x, jnp.full((8, B), i, jnp.int32), axis=0)


def columns(x):
    return [wide(x[:, j:j + 1]) for j in range(8)]


def less(x, c, w):
    t = [c[j] * w[j] for j in range(8)]
    return x - (((t[0] + t[1]) + (t[2] + t[3])) + ((t[4] + t[5]) + (t[6] + t[7])))


def diag_inverse(d, a_ref, w_ref, v_ref):
    sub = lax.broadcasted_iota(jnp.int32, (8, B), 0)
    lane = lax.broadcasted_iota(jnp.int32, (8, B), 1)
    done = lane >= B - 8
    unit = jnp.where(lane - (B - 8) == sub, 1.0, 0.0)
    a_ref[...] = pltpu.roll(d, 8, 1)
    w_ref[...] = jnp.zeros_like(w_ref)

    def shift(x):
        return jnp.where(done, 0.0, pltpu.roll(x, B - 8, 1))

    def panel(last, p, carry):
        v, v1 = carry
        zap = done & (p > 0)
        a2 = a_ref[16:24, :]
        c, t1, c2 = [], [], []
        c = columns(v)
        y = jnp.where(done, unit, pltpu.roll(v, B - 8, 1))
        for j in range(8):
            t1.append(wide(v1[:, j:j + 1]))
            c2.append(wide(a2[:, j:j + 1]))
        r1 = shift(v1)
        s = [[pick(c[j], i) if i >= j else None for j in range(8)] for i in range(8)]
        y = [wide(y[j:j + 1, :]) for j in range(8)]
        w = [wide(w_ref[j:j + 1, :]) for j in range(8)]
        x2 = less(jnp.where(zap, 0.0, pltpu.roll(a2, B - 8, 1)), c2, w)
        r = [None] * 8
        inv = [[None] * 8 for _ in range(8)]
        for j in range(8):
            r[j] = lax.rsqrt(s[j][j])
            for i in range(j + 1, 8):
                s[i][j] = s[i][j] * r[j]
            for k in range(j + 1, 8):
                for i in range(k, 8):
                    s[i][k] = s[i][k] - s[i][j] * s[k][j]
            y[j] = y[j] * r[j]
            t1[j] = t1[j] * r[j]
            for i in range(j + 1, 8):
                y[i] = y[i] - s[i][j] * y[j]
                t1[i] = t1[i] - s[i][j] * t1[j]
            for k in range(j):
                inv[j][k] = inv[j][k] * r[j]
            inv[j][j] = r[j]
            for i in range(j + 1, 8):
                for k in range(j + 1):
                    m = s[i][j] * inv[j][k]
                    inv[i][k] = -m if inv[i][k] is None else inv[i][k] - m
        bulk = a_ref[24:8 * last, :]
        change = lax.dot_general(bulk[:, :KW], w_ref[:KW, :], (((1,), (0,)), ((), ())),
            precision=lax.Precision.HIGHEST, preferred_element_type=jnp.float32)
        moved = pltpu.roll(bulk, B - 8, 1)
        far = lax.broadcasted_iota(jnp.int32, bulk.shape, 1) >= B - 8
        moved = jnp.where(far & (p > 0), 0.0, moved)
        a_ref[16:8 * last - 8, :] = moved - change
        c2 = columns(x2)
        nv = less(r1, t1, y)
        w = []
        for j in range(8):
            w.append(inv[j][j] * y[j])
            for i in range(j + 1, 8):
                w[j] = w[j] + inv[i][j] * y[i]
            w_ref[j:j + 1, :] = w[j][:1]
        nv1 = less(shift(x2), c2, w)
        rows = y[0]
        for j in range(1, 8):
            rows = jnp.where(sub == j, y[j], rows)
        v_ref[pl.ds(pl.multiple_of(p * 8, 8), 8), :] = rows
        return nv, nv1

    carry = d[0:8, :], d[8:16, :]
    for n in range(0, 16, STEP):
        carry = lax.fori_loop(n, n + STEP, functools.partial(panel, max(16 - n, 3)), carry)
    rows = lax.broadcasted_iota(jnp.int32, (B, B), 0)
    cols = lax.broadcasted_iota(jnp.int32, (B, B), 1)
    turned = [pltpu.roll(v_ref[8 * p:8 * p + 8, :], (8 * p + 8) % B, 1) for p in range(16)]
    return jnp.where(cols <= rows, jnp.concatenate(turned, axis=0), 0.0)


def after(k, inv, s_ref, hi_ref, lo_ref):
    k0, k1 = k * B, k * B + B
    if k1 < PIV:
        for j in range(k + 1, NB):
            s_ref[k0:k1, j * B:j * B + B] = jnp.zeros((B, B), jnp.float32)
        x = mm(split(s_ref[k1:, k0:k1]), split(inv))
        s_ref[k1:, k0:k1] = x
        h, l = split(x)
        hi_ref[k1:, :] = h
        lo_ref[k1:, :] = l
        for j in range(k + 1, NB):
            j0 = j * B
            s_ref[j0:, j0:j0 + B] = s_ref[j0:, j0:j0 + B] - mm(
                (hi_ref[j0:, :], lo_ref[j0:, :]), (hi_ref[j0:j0 + B, :], lo_ref[j0:j0 + B, :]))


def factor_steps(k_from, k_to, s_ref, dinv_ref, hi_ref, lo_ref, a_ref, w_ref, v_ref):
    rows = lax.broadcasted_iota(jnp.int32, (B, B), 0)
    cols = lax.broadcasted_iota(jnp.int32, (B, B), 1)

    def step(k, _):
        at = pl.ds(pl.multiple_of(k * B, B), B)
        d = s_ref[at, at]
        inv = diag_inverse(d, a_ref, w_ref, v_ref)
        dinv_ref[k] = inv
        own = lax.dot_general(d, inv, DN, precision=lax.Precision.HIGHEST, preferred_element_type=jnp.float32)
        s_ref[at, at] = jnp.where(cols <= rows, own, 0.0)
        for i in range(k_from, k_to):
            @pl.when(k == i)
            def _():
                after(i, inv, s_ref, hi_ref, lo_ref)
        return 0

    lax.fori_loop(k_from, k_to, step, 0)


def blocks_of(me):
    y, c = me // 2, me % 2
    return [2 * ((y + d) % NY) + c for d in (0, NY - 1, 1, 2)], [2 * ((y + d) % NY) + 1 - c for d in (0, NY - 1, 1, 2)]


def row_slice(block):
    return pl.ds(pl.multiple_of(block * B, B), B)


def put_pieces(dst_ref, refs, blocks):
    for ref, block in zip(refs[:3], blocks[:3]):
        dst_ref[row_slice(block), :] = ref[...]
    half = B // 2
    for n in range(2):
        dst_ref[pl.ds(pl.multiple_of(blocks[3] * B + n * half, half), half), :] = refs[3 + n][...]


def first_kernel(meta_ref, hold_ref, *refs):
    pieces, (s_ref, dinv_ref, tok_ref), (g_ref, *scratch) = refs[:10], refs[10:13], refs[13:]
    own, other = blocks_of(meta_ref[0])
    put_pieces(g_ref, pieces[:5], own)
    put_pieces(g_ref, pieces[5:], other)
    for i in range(NB):
        for j in range(i + 1):
            d = i - j
            if d < SLOTS:
                block = g_ref[i * B:i * B + B, d * B:d * B + B]
            else:
                t = NB - d
                block = g_ref[j * B:j * B + B, t * B:t * B + B].T
            s_ref[i * B:i * B + B, j * B:j * B + B] = block
    factor_steps(0, CUT, s_ref, dinv_ref, *scratch)
    tok_ref[...] = hold_ref[...]


def second_kernel(s_in, dinv_in, tok_in, s_ref, dinv_ref, tok_ref, *scratch):
    factor_steps(CUT, NB, s_ref, dinv_ref, *scratch)
    tok_ref[...] = tok_in[...]


def chol_scratch():
    return [
        pltpu.VMEM((PIV, B), jnp.bfloat16),
        pltpu.VMEM((PIV, B), jnp.bfloat16),
        pltpu.VMEM((B, B), jnp.float32),
        pltpu.VMEM((B, B), jnp.float32),
        pltpu.VMEM((B, B), jnp.float32),
    ]


VM = pl.BlockSpec(memory_space=pltpu.VMEM)
SM = pl.BlockSpec(memory_space=pltpu.SMEM)
FACTOR = (
    jax.ShapeDtypeStruct((PIV, PIV), jnp.float32),
    jax.ShapeDtypeStruct((NB, B, B), jnp.float32),
    jax.ShapeDtypeStruct((8, B), jnp.float32),
)


def cost(flops):
    return pl.CostEstimate(flops=flops, bytes_accessed=4 * MIB, transcendentals=0)


def chol_first(meta, hold, pieces):
    return pl.pallas_call(
        first_kernel,
        in_specs=[SM] + [VM] * 11,
        out_shape=FACTOR,
        scratch_shapes=[pltpu.VMEM((PIV, SLOTS * B), jnp.float32)] + chol_scratch(),
        compiler_params=pltpu.CompilerParams(vmem_limit_bytes=18 * MIB),
        cost_estimate=cost(20 * 10**9),
        name="chol_first",
    )(meta, jnp.broadcast_to(hold, (8, B)), *pieces)


def chol_second(s, dinv, tok):
    return pl.pallas_call(
        second_kernel,
        in_specs=[VM] * 3,
        out_shape=FACTOR,
        scratch_shapes=chol_scratch(),
        input_output_aliases={0: 0, 1: 1},
        compiler_params=pltpu.CompilerParams(vmem_limit_bytes=18 * MIB),
        cost_estimate=cost(20 * 10**9),
        name="chol_second",
    )(s, dinv, tok)


def solve_kernel(meta_ref, l_ref, dinv_ref, x0, x1, x2, x3, x4, x_ref, fac_ref, xh_ref, xl_ref):
    keep = meta_ref[9] > 0
    for k in range(NB):
        k0, k1 = k * B, k * B + B
        c = jnp.concatenate([r[:, k0:k1] for r in (x0, x1, x2, x3, x4)], axis=0)
        if k > 0:
            c = c - mm((xh_ref[:, :k0], xl_ref[:, :k0]), split(l_ref[k0:k1, :k0]))
        x = mm(split(c), split(dinv_ref[k]))
        x_ref[:, k0:k1] = x
        fac_ref[1, :, k0:k1] = jnp.where(keep, x[:B], 0.0)
        h, l = split(x)
        xh_ref[:, k0:k1] = h
        xl_ref[:, k0:k1] = l
    fac_ref[0] = jnp.where(keep, l_ref[row_slice(meta_ref[0]), :], 0.0)


def solve(meta, s, dinv, pieces):
    return pl.pallas_call(
        solve_kernel,
        in_specs=[SM] + [VM] * 7,
        out_shape=(
            jax.ShapeDtypeStruct((PIV // 2, PIV), jnp.float32),
            jax.ShapeDtypeStruct((2, B, PIV), jnp.float32),
        ),
        scratch_shapes=[pltpu.VMEM((PIV // 2, PIV), jnp.bfloat16)] * 2,
        compiler_params=pltpu.CompilerParams(vmem_limit_bytes=20 * MIB),
        cost_estimate=cost(3 * 10**9),
        name="solve",
    )(meta, s, dinv, *pieces)


def child_kernel(meta_ref, x_ref, xp_ref, g_ref, ec_ref, ep_ref, er_ref, xh_ref, xl_ref, rr_ref):
    me = meta_ref[0]
    own, other = blocks_of(me)
    for a in range(NB):
        for b in range(NB):
            t = (a - b) % NB
            block = g_ref[a, :, t * B:t * B + B] if t < SLOTS else g_ref[b, :, (NB - t) * B:(NB - t) * B + B].T
            rr_ref[a * B:a * B + B, b * B:b * B + B] = block
    for n in range(NY):
        for blocks, ref in ((own, x_ref), (other, xp_ref)):
            h, l = split(ref[n * B:n * B + B, :])
            xh_ref[row_slice(blocks[n]), :] = h
            xl_ref[row_slice(blocks[n]), :] = l
    x = (xh_ref[...], xl_ref[...])
    for half in range(2):
        a = jnp.int32(-1)
        for b in range(NB):
            a = jnp.where(meta_ref[1 + b] == me + half * NB, b, a)
        held = a >= 0
        at = row_slice(jnp.maximum(a, 0))
        u = rr_ref[at, :] - mm((xh_ref[at, :], xl_ref[at, :]), x)
        u = jnp.where(held, u, 0.0)
        for out_ref in (ec_ref,) if half == 0 else (ep_ref, er_ref):
            out_ref[...] = jnp.zeros_like(out_ref)
        for b in range(NB):
            to = meta_ref[1 + b]
            part = u[:, b * B:b * B + B]
            if half == 0:
                slot = (me - to) % NB

                @pl.when((to < NB) & (slot < SLOTS))
                def _():
                    ec_ref[:, row_slice(jnp.minimum(slot, SLOTS - 1))] = part
            else:
                for out_ref, hit in ((ep_ref, to < NB), (er_ref, to >= NB)):
                    @pl.when(hit)
                    def _():
                        out_ref[:, row_slice(to % NB)] = part


def child_update(meta, x, xp, rr):
    return pl.pallas_call(
        child_kernel,
        in_specs=[SM] + [VM] * 3,
        out_shape=tuple(jax.ShapeDtypeStruct((B, n * B), jnp.float32) for n in (SLOTS, NB, NB)),
        scratch_shapes=[pltpu.VMEM((PIV, PIV), jnp.bfloat16)] * 2 + [pltpu.VMEM((PIV, PIV), jnp.float32)],
        compiler_params=pltpu.CompilerParams(vmem_limit_bytes=24 * MIB),
        cost_estimate=cost(3 * 10**9),
        name="child_update",
    )(meta, x, xp, rr)


def parent_kernel(meta_ref, x_ref, xp_ref, rr_ref, cb_ref):
    keep = meta_ref[9] > 0
    own, other = blocks_of(meta_ref[0])
    mine = split(x_ref[:B, :])
    for blocks, ref in ((own, x_ref), (other, xp_ref)):
        prod = mm(mine, split(ref[...]))
        for n in range(NY):
            at = row_slice(blocks[n])
            cb_ref[:, at] = jnp.where(keep, rr_ref[:, at] - prod[:, n * B:n * B + B], 0.0)


def parent_update(meta, x, xp, rr):
    return pl.pallas_call(
        parent_kernel,
        in_specs=[SM] + [VM] * 3,
        out_shape=jax.ShapeDtypeStruct((B, PIV), jnp.float32),
        compiler_params=pltpu.CompilerParams(vmem_limit_bytes=16 * MIB),
        cost_estimate=cost(10**9),
        name="parent_update",
    )(meta, x, xp, rr)


def pick_kernel(meta_ref, *refs):
    me = meta_ref[0]
    n = len(refs) // 2
    for row_ref, out_ref in zip(refs[:n], refs[n:]):
        for t in range(SLOTS):
            out_ref[:, t * B:t * B + B] = row_ref[:, row_slice((me + NB - t) % NB)]


def pick_slots(meta, front, n):
    return pl.pallas_call(
        pick_kernel,
        grid=(1,),
        in_specs=[SM] + [pl.BlockSpec((None, None, None, B, PIV), lambda g, i=i: (0, i, 0, 0, i)) for i in range(n)],
        out_specs=[pl.BlockSpec((B, SLOTS * B), lambda g: (0, 0))] * n,
        out_shape=[jax.ShapeDtypeStruct((B, SLOTS * B), jnp.float32)] * n,
        cost_estimate=pl.CostEstimate(flops=0, bytes_accessed=n * MIB, transcendentals=0),
        name="pick_slots",
    )(meta, *([front] * n))


def along_y(x, d):
    return lax.ppermute(x, "rows", [(i, (i + 2 * d) % NB) for i in range(NB)])


def to_partner(x):
    return lax.ppermute(x, "rows", [(i, i ^ 1) for i in range(NB)])


def from_right(x, shift):
    leaves = lax.axis_size("leaf")
    return lax.ppermute(x, "leaf", [(i + shift, i) for i in range(leaves - shift)])


def zero_of(x):
    return jnp.minimum(jnp.abs(x[:1, :1]), 0.0)


def gather_pivots(x):
    below, above = along_y(x, 1), along_y(x, -1)
    half = B // 2
    far0, far1 = along_y(below[:half], 1), along_y(above[half:], -1)
    pieces = [x, below, above, far0, far1]
    return pieces + [to_partner(p) for p in pieces]


def far_halves(below, above, after):
    half = B // 2
    return below[:half] + after, above[half:] + after


def two_levels(child_front_entries, parent_fronts, parent_of, positions):
    me = lax.axis_index("rows")
    leaf = lax.axis_index("leaf")
    low_child, low_parent = child_front_entries[0, 1, 0], parent_fronts[0, 1, 0]

    padded = jnp.concatenate([jnp.full((1,), -1, jnp.int32), parent_of, jnp.full((2,), -1, jnp.int32)])
    near = lax.dynamic_slice(padded, (leaf,), (4,))
    head = near[1] != near[0]
    same1, same2 = near[1] == near[2], near[1] == near[3]
    me1 = me.astype(jnp.int32)[None]
    meta_c = jnp.concatenate([me1, positions[0], jnp.ones((1,), jnp.int32)])
    meta_p = jnp.concatenate([me1, positions[0], head.astype(jnp.int32)[None]])

    def add(x, got, same):
        return x + jnp.where(same, got, 0.0)

    own_slots, low_slots = pick_slots(meta_c, child_front_entries, 2)
    pieces = gather_pivots(own_slots)
    begun = zero_of(pieces[-1]) + zero_of(pieces[-2])
    rp = low_child[:, :PIV] + begun
    low_slots = low_slots + begun
    rr = lax.all_gather(low_slots, "rows")
    rp_b, rp_a = along_y(rp, 1), along_y(rp, -1)
    s, dinv, tok = chol_first(meta_c, zero_of(low_slots), pieces)
    half0, half1 = far_halves(rp_b, rp_a, tok[:1, :1])
    rp_f = along_y(half0, 1), along_y(half1, -1)
    s, dinv, tok = chol_second(s, dinv, tok + (zero_of(half0) + zero_of(half1)))
    x, child_out = solve(meta_c, s, dinv, [rp, rp_b, rp_a, *rp_f])
    xp = to_partner(x)
    ext_c, ext_p, ext_r = child_update(meta_c, x, xp, rr)

    sum_c = add(ext_c, from_right(ext_c, 1), same1)
    sum_c = add(sum_c, from_right(sum_c, 2), same2)
    pivots = pick_slots(meta_c, parent_fronts, 1)[0] + sum_c
    pieces = gather_pivots(pivots)
    ext_p = ext_p + zero_of(pivots)
    sum_p = add(ext_p, from_right(ext_p, 1), same1)
    got_p = from_right(sum_p, 2)
    s, dinv, tok = chol_first(meta_p, zero_of(sum_p), pieces)
    z = tok[:1, :1]
    rp = low_parent[:, :PIV] + add(sum_p, got_p + z, same2)
    rp_b, rp_a = along_y(rp, 1), along_y(rp, -1)
    ext_r = ext_r + z
    got_r = from_right(ext_r, 1)
    s, dinv, tok = chol_second(s, dinv, tok + (zero_of(rp) + zero_of(ext_r)))
    z = tok[:1, :1]
    half0, half1 = far_halves(rp_b, rp_a, z)
    rp_f = along_y(half0, 1), along_y(half1, -1)
    sum_r = add(ext_r, got_r + z, same1)
    got_r = from_right(sum_r, 2)
    x, parent_out = solve(meta_p, s, dinv, [rp, rp_b, rp_a, *rp_f])
    xp = to_partner(x)
    rr = low_parent[:, PIV:] + add(sum_r, got_r, same2)
    block_out = parent_update(meta_p, x, xp, rr)
    return (
        child_out[None, :, None],
        parent_out[None, :, None],
        block_out[None, None, None],
    )


def solution(mesh):
    placed = P("leaf", None, "rows", None, None)
    return jax.shard_map(
        two_levels,
        mesh=mesh,
        in_specs=(placed, placed, P(), P("leaf", None)),
        out_specs=(placed, placed, placed),
        check_vma=False,
    )
```

```python
import functools

import jax
import jax.numpy as jnp
from jax import lax
from jax.experimental import pallas as pl
from jax.experimental.pallas import tpu as pltpu
from jax.sharding import PartitionSpec as P


B = 128
PIV = 1024
NB = PIV // B
NY = NB // 2
SLOTS = 5
CUT = 5
KW = 16
STEP = 8
MIB = 2**20
DN = (((1,), (1,)), ((), ()))


def split(x):
    hi = x.astype(jnp.bfloat16)
    lo = (x - hi.astype(jnp.float32)).astype(jnp.bfloat16)
    return hi, lo


def dot(a, b):
    return lax.dot_general(a, b, DN, preferred_element_type=jnp.float32)


def mm(a, b):
    (ah, al), (bh, bl) = a, b
    return dot(ah, bh) + (dot(ah, bl) + dot(al, bh))


def wide(x):
    return jnp.broadcast_to(x, (8, B))


def sublane(x, i):
    return jnp.take_along_axis(x, jnp.full((8, B), i, jnp.int32), axis=0)


def columns(x):
    return [wide(x[:, j:j + 1]) for j in range(8)]


def less(x, c, w):
    t = [c[j] * w[j] for j in range(8)]
    return x - (((t[0] + t[1]) + (t[2] + t[3])) + ((t[4] + t[5]) + (t[6] + t[7])))


def diag_inverse(d, a_ref, w_ref, v_ref):
    sub = lax.broadcasted_iota(jnp.int32, (8, B), 0)
    lane = lax.broadcasted_iota(jnp.int32, (8, B), 1)
    done = lane >= B - 8
    unit = jnp.where(lane - (B - 8) == sub, 1.0, 0.0)
    a_ref[...] = pltpu.roll(d, 8, 1)
    w_ref[...] = jnp.zeros_like(w_ref)

    def shift(x):
        return jnp.where(done, 0.0, pltpu.roll(x, B - 8, 1))

    def panel(last, p, carry):
        v, v1 = carry
        zap = done & (p > 0)
        a2 = a_ref[16:24, :]
        c, t1, c2 = [], [], []
        c = columns(v)
        y = jnp.where(done, unit, pltpu.roll(v, B - 8, 1))
        for j in range(8):
            t1.append(wide(v1[:, j:j + 1]))
            c2.append(wide(a2[:, j:j + 1]))
        r1 = shift(v1)
        s = [[sublane(c[j], i) if i >= j else None for j in range(8)] for i in range(8)]
        y = [wide(y[j:j + 1, :]) for j in range(8)]
        w = [wide(w_ref[j:j + 1, :]) for j in range(8)]
        x2 = less(jnp.where(zap, 0.0, pltpu.roll(a2, B - 8, 1)), c2, w)
        r = [None] * 8
        inv = [[None] * 8 for _ in range(8)]
        for j in range(8):
            r[j] = lax.rsqrt(s[j][j])
            for i in range(j + 1, 8):
                s[i][j] = s[i][j] * r[j]
            for k in range(j + 1, 8):
                for i in range(k, 8):
                    s[i][k] = s[i][k] - s[i][j] * s[k][j]
            y[j] = y[j] * r[j]
            t1[j] = t1[j] * r[j]
            for i in range(j + 1, 8):
                y[i] = y[i] - s[i][j] * y[j]
                t1[i] = t1[i] - s[i][j] * t1[j]
            for k in range(j):
                inv[j][k] = inv[j][k] * r[j]
            inv[j][j] = r[j]
            for i in range(j + 1, 8):
                for k in range(j + 1):
                    m = s[i][j] * inv[j][k]
                    inv[i][k] = -m if inv[i][k] is None else inv[i][k] - m
        bulk = a_ref[24:8 * last, :]
        change = lax.dot_general(bulk[:, :KW], w_ref[:KW, :], (((1,), (0,)), ((), ())),
            precision=lax.Precision.HIGHEST, preferred_element_type=jnp.float32)
        moved = pltpu.roll(bulk, B - 8, 1)
        far = lax.broadcasted_iota(jnp.int32, bulk.shape, 1) >= B - 8
        moved = jnp.where(far & (p > 0), 0.0, moved)
        a_ref[16:8 * last - 8, :] = moved - change
        c2 = columns(x2)
        nv = less(r1, t1, y)
        w = []
        for j in range(8):
            w.append(inv[j][j] * y[j])
            for i in range(j + 1, 8):
                w[j] = w[j] + inv[i][j] * y[i]
            w_ref[j:j + 1, :] = w[j][:1]
        nv1 = less(shift(x2), c2, w)
        rows = y[0]
        for j in range(1, 8):
            rows = jnp.where(sub == j, y[j], rows)
        v_ref[pl.ds(pl.multiple_of(p * 8, 8), 8), :] = rows
        return nv, nv1

    carry = d[0:8, :], d[8:16, :]
    for n in range(0, 16, STEP):
        carry = lax.fori_loop(n, n + STEP, functools.partial(panel, max(16 - n, 3)), carry)
    rows = lax.broadcasted_iota(jnp.int32, (B, B), 0)
    cols = lax.broadcasted_iota(jnp.int32, (B, B), 1)
    turned = [pltpu.roll(v_ref[8 * p:8 * p + 8, :], (8 * p + 8) % B, 1) for p in range(16)]
    return jnp.where(cols <= rows, jnp.concatenate(turned, axis=0), 0.0)


def after(k, inv, s_ref, hi_ref, lo_ref):
    k0, k1 = k * B, k * B + B
    if k1 < PIV:
        for j in range(k + 1, NB):
            s_ref[k0:k1, j * B:j * B + B] = jnp.zeros((B, B), jnp.float32)
        x = mm(split(s_ref[k1:, k0:k1]), split(inv))
        s_ref[k1:, k0:k1] = x
        h, l = split(x)
        hi_ref[k1:, :] = h
        lo_ref[k1:, :] = l
        for j in range(k + 1, NB):
            j0 = j * B
            s_ref[j0:, j0:j0 + B] = s_ref[j0:, j0:j0 + B] - mm(
                (hi_ref[j0:, :], lo_ref[j0:, :]), (hi_ref[j0:j0 + B, :], lo_ref[j0:j0 + B, :]))


def factor_steps(k_from, k_to, s_ref, dinv_ref, hi_ref, lo_ref, a_ref, w_ref, v_ref):
    rows = lax.broadcasted_iota(jnp.int32, (B, B), 0)
    cols = lax.broadcasted_iota(jnp.int32, (B, B), 1)

    def step(k, _):
        at = pl.ds(pl.multiple_of(k * B, B), B)
        d = s_ref[at, at]
        inv = diag_inverse(d, a_ref, w_ref, v_ref)
        dinv_ref[k] = inv
        own = lax.dot_general(d, inv, DN, precision=lax.Precision.HIGHEST, preferred_element_type=jnp.float32)
        s_ref[at, at] = jnp.where(cols <= rows, own, 0.0)
        for i in range(k_from, k_to):
            @pl.when(k == i)
            def _():
                after(i, inv, s_ref, hi_ref, lo_ref)
        return 0

    lax.fori_loop(k_from, k_to, step, 0)


def blocks_of(me):
    y, c = me // 2, me % 2
    near, far, across = (y + 3 - 2 * c) % NY, (y + 2) % NY, (y + 1 + 2 * c) % NY
    own = [2 * y + c, 2 * near + c, 2 * near + 1 - c, 2 * far + c]
    other = [2 * y + 1 - c, 2 * across + 1 - c, 2 * across + c, 2 * far + 1 - c]
    return own, other


def row_slice(block):
    return pl.ds(pl.multiple_of(block * B, B), B)


def fetch(pairs, sems):
    copies = [pltpu.make_async_copy(src, dst, sems.at[n]) for n, (src, dst) in enumerate(pairs)]
    for copy in copies:
        copy.start()
    return copies


def first_kernel(*refs):
    pieces, (s_ref, dinv_ref), (g_ref, sems, *scratch) = refs[:8], refs[8:10], refs[10:]
    own, other = blocks_of(lax.axis_index("rows"))
    for copy in fetch([(r, g_ref.at[row_slice(n), :]) for r, n in zip(pieces, own + other)], sems):
        copy.wait()
    for i in range(NB):
        for j in range(i + 1):
            d = i - j
            if d < SLOTS:
                block = g_ref[i * B:i * B + B, d * B:d * B + B]
            else:
                t = NB - d
                block = g_ref[j * B:j * B + B, t * B:t * B + B].T
            s_ref[i * B:i * B + B, j * B:j * B + B] = block
    factor_steps(0, CUT, s_ref, dinv_ref, *scratch)


def second_kernel(s_in, dinv_in, s_ref, dinv_ref, *scratch):
    factor_steps(CUT, NB, s_ref, dinv_ref, *scratch)


def chol_scratch():
    return [
        pltpu.VMEM((PIV, B), jnp.bfloat16),
        pltpu.VMEM((PIV, B), jnp.bfloat16),
        pltpu.VMEM((B, B), jnp.float32),
        pltpu.VMEM((B, B), jnp.float32),
        pltpu.VMEM((B, B), jnp.float32),
    ]


VM = pl.BlockSpec(memory_space=pltpu.VMEM)
SM = pl.BlockSpec(memory_space=pltpu.SMEM)
ANY = pl.BlockSpec(memory_space=pl.ANY)
FACTOR = (
    jax.ShapeDtypeStruct((PIV, PIV), jnp.float32),
    jax.ShapeDtypeStruct((NB, B, B), jnp.float32),
)


def cost(flops):
    return pl.CostEstimate(flops=flops, bytes_accessed=4 * MIB, transcendentals=0)


def chol_first(pieces):
    return pl.pallas_call(
        first_kernel,
        in_specs=[ANY] * 8,
        out_shape=FACTOR,
        scratch_shapes=[pltpu.VMEM((PIV, SLOTS * B), jnp.float32), pltpu.SemaphoreType.DMA((8,))] + chol_scratch(),
        compiler_params=pltpu.CompilerParams(vmem_limit_bytes=18 * MIB),
        cost_estimate=cost(20 * 10**9),
        name="chol_first",
    )(*pieces)


def chol_second(s, dinv):
    return pl.pallas_call(
        second_kernel,
        in_specs=[VM] * 2,
        out_shape=FACTOR,
        scratch_shapes=chol_scratch(),
        input_output_aliases={0: 0, 1: 1},
        compiler_params=pltpu.CompilerParams(vmem_limit_bytes=18 * MIB),
        cost_estimate=cost(20 * 10**9),
        name="chol_second",
    )(s, dinv)


def solve_kernel(keep_ref, l_ref, dinv_ref, x0, x1, x2, x3, x_ref, fac_ref, c_ref, xh_ref, xl_ref, sems):
    copies = fetch([(r, c_ref.at[n * B:n * B + B, :]) for n, r in enumerate((x0, x1, x2, x3))], sems)
    keep = keep_ref[0] > 0
    fac_ref[0] = jnp.where(keep, l_ref[row_slice(lax.axis_index("rows")), :], 0.0)
    for copy in copies:
        copy.wait()
    for k in range(NB):
        k0, k1 = k * B, k * B + B
        c = c_ref[:, k0:k1]
        if k > 0:
            c = c - mm((xh_ref[:, :k0], xl_ref[:, :k0]), split(l_ref[k0:k1, :k0]))
        x = mm(split(c), split(dinv_ref[k]))
        x_ref[:, k0:k1] = x
        fac_ref[1, :, k0:k1] = jnp.where(keep, x[:B], 0.0)
        h, l = split(x)
        xh_ref[:, k0:k1] = h
        xl_ref[:, k0:k1] = l


def solve(keep, s, dinv, pieces):
    return pl.pallas_call(
        solve_kernel,
        in_specs=[SM] + [VM] * 2 + [ANY] * 4,
        out_shape=(
            jax.ShapeDtypeStruct((PIV // 2, PIV), jnp.float32),
            jax.ShapeDtypeStruct((2, B, PIV), jnp.float32),
        ),
        scratch_shapes=[pltpu.VMEM((PIV // 2, PIV), jnp.float32)]
        + [pltpu.VMEM((PIV // 2, PIV), jnp.bfloat16)] * 2
        + [pltpu.SemaphoreType.DMA((4,))],
        compiler_params=pltpu.CompilerParams(vmem_limit_bytes=20 * MIB),
        cost_estimate=cost(3 * 10**9),
        name="solve",
    )(keep, s, dinv, *pieces)


def child_kernel(pos_ref, x_in, xp_in, rr_in, ec_ref, ep_ref, er_ref, x_ref, g_ref, rr_ref, xh_ref, xl_ref, sems):
    me = lax.axis_index("rows")
    half = PIV // 2
    copies = fetch([(rr_in, g_ref), (x_in, x_ref.at[:half, :]), (xp_in, x_ref.at[half:, :])], sems)
    copies[0].wait()
    for a in range(NB):
        for b in range(NB):
            t, u = (a - b) % NB, (b - a) % NB
            block = g_ref[a * B:a * B + B, t * B:t * B + B] if t < SLOTS else g_ref[b * B:b * B + B, u * B:u * B + B].T
            rr_ref[a * B:a * B + B, b * B:b * B + B] = block
    copies[1].wait()
    copies[2].wait()
    own, other = blocks_of(me)
    for n, block in enumerate(own + other):
        h, l = split(x_ref[n * B:n * B + B, :])
        xh_ref[row_slice(block), :] = h
        xl_ref[row_slice(block), :] = l
    x = (xh_ref[...], xl_ref[...])
    for half in range(2):
        a = jnp.int32(-1)
        for b in range(NB):
            a = jnp.where(pos_ref[b] == me + half * NB, b, a)
        held = a >= 0
        at = row_slice(jnp.maximum(a, 0))
        u = rr_ref[at, :] - mm((xh_ref[at, :], xl_ref[at, :]), x)
        u = jnp.where(held, u, 0.0)
        for out_ref in (ec_ref,) if half == 0 else (ep_ref, er_ref):
            out_ref[...] = jnp.zeros_like(out_ref)
        for b in range(NB):
            to = pos_ref[b]
            part = u[:, b * B:b * B + B]
            if half == 0:
                slot = (me - to) % NB

                @pl.when((to < NB) & (slot < SLOTS))
                def _():
                    ec_ref[:, row_slice(jnp.minimum(slot, SLOTS - 1))] = part
            else:
                for out_ref, hit in ((ep_ref, to < NB), (er_ref, to >= NB)):
                    @pl.when(hit)
                    def _():
                        out_ref[:, row_slice(to % NB)] = part


def child_update(positions, x, xp, rr):
    return pl.pallas_call(
        child_kernel,
        in_specs=[SM] + [ANY] * 3,
        out_shape=tuple(jax.ShapeDtypeStruct((B, n * B), jnp.float32) for n in (SLOTS, NB, NB)),
        scratch_shapes=[
            pltpu.VMEM((PIV, PIV), jnp.float32),
            pltpu.VMEM((PIV, SLOTS * B), jnp.float32),
            pltpu.VMEM((PIV, PIV), jnp.float32),
            pltpu.VMEM((PIV, PIV), jnp.bfloat16),
            pltpu.VMEM((PIV, PIV), jnp.bfloat16),
            pltpu.SemaphoreType.DMA((3,)),
        ],
        compiler_params=pltpu.CompilerParams(vmem_limit_bytes=56 * MIB),
        cost_estimate=cost(3 * 10**9),
        name="child_update",
    )(positions, x, xp, rr)


def parent_kernel(flags_ref, x_in, xp_in, front_in, sum_in, got_in, cb_ref, x_ref, r_ref, sems):
    half = PIV // 2
    copies = fetch(
        [(x_in, x_ref.at[:half, :]), (xp_in, x_ref.at[half:, :]), (front_in.at[0, 1, 0, :, PIV:], r_ref.at[0])]
        + [(sum_in, r_ref.at[1]), (got_in, r_ref.at[2])],
        sems,
    )
    keep, same = flags_ref[0] > 0, flags_ref[1] > 0
    own, other = blocks_of(lax.axis_index("rows"))
    for copy in copies:
        copy.wait()
    prod = mm(split(x_ref[:B, :]), split(x_ref[...]))
    r_ref[0] = r_ref[0] + (r_ref[1] + jnp.where(same, r_ref[2], 0.0))
    for n, block in enumerate(own + other):
        at = row_slice(block)
        cb_ref[:, at] = jnp.where(keep, r_ref[0, :, at] - prod[:, n * B:n * B + B], 0.0)


def parent_update(flags, x, xp, front, sum_r, got):
    return pl.pallas_call(
        parent_kernel,
        in_specs=[SM] + [ANY] * 5,
        out_shape=jax.ShapeDtypeStruct((B, PIV), jnp.float32),
        scratch_shapes=[
            pltpu.VMEM((PIV, PIV), jnp.float32),
            pltpu.VMEM((3, B, PIV), jnp.float32),
            pltpu.SemaphoreType.DMA((5,)),
        ],
        compiler_params=pltpu.CompilerParams(vmem_limit_bytes=56 * MIB),
        cost_estimate=cost(10**9),
        name="parent_update",
    )(flags, x, xp, front, sum_r, got)


def pick(row_ref, out_ref):
    me = lax.axis_index("rows")
    for t in range(SLOTS):
        out_ref[:, t * B:t * B + B] = row_ref[:, row_slice((me + NB - t) % NB)]


def child_pieces_kernel(top_ref, low_ref, rest_ref, pp_ref, rp_ref, rr_ref):
    pick(top_ref, pp_ref)
    pick(rest_ref, rr_ref)
    rp_ref[...] = low_ref[...]


def parent_pieces_kernel(top_ref, pp_ref):
    pick(top_ref, pp_ref)


def pieces_of(kernel, front, quarters, widths):
    return pl.pallas_call(
        kernel,
        grid=(1,),
        in_specs=[pl.BlockSpec((None, None, None, B, PIV), lambda g, i=i, j=j: (0, i, 0, 0, j)) for i, j in quarters],
        out_specs=[pl.BlockSpec((B, n * B), lambda g: (0, 0)) for n in widths],
        out_shape=[jax.ShapeDtypeStruct((B, n * B), jnp.float32) for n in widths],
        cost_estimate=pl.CostEstimate(flops=0, bytes_accessed=MIB, transcendentals=0),
    )(*([front] * len(quarters)))


def to_next(x):
    return lax.ppermute(x, "rows", [(i, (i + 2 - 4 * (i % 2)) % NB) for i in range(NB)])


def to_partner(x):
    return lax.ppermute(x, "rows", [(i, i ^ 1) for i in range(NB)])


def from_right(x, shift):
    leaves = lax.axis_size("leaf")
    return lax.ppermute(x, "leaf", [(i + shift, i) for i in range(leaves - shift)])


def two_levels(child_front_entries, parent_fronts, parent_of, positions):
    leaf = lax.axis_index("leaf")
    padded = jnp.concatenate([jnp.full((1,), -1, jnp.int32), parent_of, jnp.full((2,), -1, jnp.int32)])
    near = lax.dynamic_slice(padded, (leaf,), (4,))
    head = (near[1:2] != near[0:1]).astype(jnp.int32)
    same1, same2 = near[1] == near[2], near[1] == near[3]
    every = jnp.ones((1,), jnp.int32)

    def add(x, got, same):
        return x + jnp.where(same, got, 0.0)

    def gather_pivots(x):
        across = to_partner(x)
        one = to_next(x)
        two = to_next(across)
        far = to_next(one)
        mine = [x, one, two, far]
        return mine + [across, to_partner(one), to_partner(two), to_partner(far)]

    pp, rp, rest = pieces_of(child_pieces_kernel, child_front_entries, ((0, 0), (1, 0), (1, 1)), (SLOTS, NB, SLOTS))
    pieces = gather_pivots(pp)
    rr = lax.all_gather(rest, "rows", tiled=True)
    across = to_partner(rp)
    one, two = to_next(rp), to_next(across)
    s, dinv = chol_first(pieces)
    far = to_next(one)
    s, dinv = chol_second(s, dinv)
    x, child_out = solve(every, s, dinv, [rp, one, two, far])
    xp = to_partner(x)
    ext_c, ext_p, ext_r = child_update(positions[0], x, xp, rr)

    sum_c = add(ext_c, from_right(ext_c, 1), same1)
    got = from_right(sum_c, 2)
    sum_c = add(sum_c, got, same2)
    (pp,) = pieces_of(parent_pieces_kernel, parent_fronts, ((0, 0),), (SLOTS,))
    pieces = gather_pivots(pp + sum_c)
    got = from_right(ext_p, 1)
    sum_p = add(ext_p, got, same1)
    got = from_right(sum_p, 2)
    s, dinv = chol_first(pieces)
    rp = parent_fronts[0, 1, 0, :, :PIV] + add(sum_p, got, same2)
    across = to_partner(rp)
    one, two = to_next(rp), to_next(across)
    got = from_right(ext_r, 1)
    s, dinv = chol_second(s, dinv)
    far = to_next(one)
    sum_r = add(ext_r, got, same1)
    got = from_right(sum_r, 2)
    x, parent_out = solve(head, s, dinv, [rp, one, two, far])
    xp = to_partner(x)
    flags = jnp.concatenate([head, same2.astype(jnp.int32)[None]])
    block_out = parent_update(flags, x, xp, parent_fronts, sum_r, got)
    return (
        child_out[None, :, None],
        parent_out[None, :, None],
        block_out[None, None, None],
    )


def solution(mesh):
    placed = P("leaf", None, "rows", None, None)
    return jax.shard_map(
        two_levels,
        mesh=mesh,
        in_specs=(placed, placed, P(), P("leaf", None)),
        out_specs=(placed, placed, placed),
        check_vma=False,
    )
```

```python
import functools

import jax
import jax.numpy as jnp
from jax import lax
from jax.experimental import pallas as pl
from jax.experimental.pallas import tpu as pltpu
from jax.sharding import PartitionSpec as P


B = 128
PIV = 1024
NB = PIV // B
NY = NB // 2
SLOTS = 5
CUT = 5
KW = 16
STEP = 8
MIB = 2**20
DN = (((1,), (1,)), ((), ()))


def split(x):
    hi = x.astype(jnp.bfloat16)
    lo = (x - hi.astype(jnp.float32)).astype(jnp.bfloat16)
    return hi, lo


def dot(a, b):
    return lax.dot_general(a, b, DN, preferred_element_type=jnp.float32)


def mm(a, b):
    (ah, al), (bh, bl) = a, b
    return dot(ah, bh) + (dot(ah, bl) + dot(al, bh))


def wide(x):
    return jnp.broadcast_to(x, (8, B))


def sublane(x, i):
    return jnp.take_along_axis(x, jnp.full((8, B), i, jnp.int32), axis=0)


def columns(x):
    return [wide(x[:, j:j + 1]) for j in range(8)]


def less(x, c, w):
    t = [c[j] * w[j] for j in range(8)]
    return x - (((t[0] + t[1]) + (t[2] + t[3])) + ((t[4] + t[5]) + (t[6] + t[7])))


def diag_inverse(d, a_ref, w_ref, v_ref):
    sub = lax.broadcasted_iota(jnp.int32, (8, B), 0)
    lane = lax.broadcasted_iota(jnp.int32, (8, B), 1)
    done = lane >= B - 8
    unit = jnp.where(lane - (B - 8) == sub, 1.0, 0.0)
    a_ref[...] = pltpu.roll(d, 8, 1)
    w_ref[...] = jnp.zeros_like(w_ref)

    def shift(x):
        return jnp.where(done, 0.0, pltpu.roll(x, B - 8, 1))

    def panel(last, p, carry):
        v, v1 = carry
        zap = done & (p > 0)
        a2 = a_ref[16:24, :]
        c, t1, c2 = [], [], []
        c = columns(v)
        y = jnp.where(done, unit, pltpu.roll(v, B - 8, 1))
        for j in range(8):
            t1.append(wide(v1[:, j:j + 1]))
            c2.append(wide(a2[:, j:j + 1]))
        r1 = shift(v1)
        s = [[sublane(c[j], i) if i >= j else None for j in range(8)] for i in range(8)]
        y = [wide(y[j:j + 1, :]) for j in range(8)]
        w = [wide(w_ref[j:j + 1, :]) for j in range(8)]
        x2 = less(jnp.where(zap, 0.0, pltpu.roll(a2, B - 8, 1)), c2, w)
        r = [None] * 8
        inv = [[None] * 8 for _ in range(8)]
        for j in range(8):
            r[j] = lax.rsqrt(s[j][j])
            for i in range(j + 1, 8):
                s[i][j] = s[i][j] * r[j]
            for k in range(j + 1, 8):
                for i in range(k, 8):
                    s[i][k] = s[i][k] - s[i][j] * s[k][j]
            y[j] = y[j] * r[j]
            t1[j] = t1[j] * r[j]
            for i in range(j + 1, 8):
                y[i] = y[i] - s[i][j] * y[j]
                t1[i] = t1[i] - s[i][j] * t1[j]
            for k in range(j):
                inv[j][k] = inv[j][k] * r[j]
            inv[j][j] = r[j]
            for i in range(j + 1, 8):
                for k in range(j + 1):
                    m = s[i][j] * inv[j][k]
                    inv[i][k] = -m if inv[i][k] is None else inv[i][k] - m
        bulk = a_ref[24:8 * last, :]
        change = lax.dot_general(bulk[:, :KW], w_ref[:KW, :], (((1,), (0,)), ((), ())),
            precision=lax.Precision.HIGHEST, preferred_element_type=jnp.float32)
        moved = pltpu.roll(bulk, B - 8, 1)
        far = lax.broadcasted_iota(jnp.int32, bulk.shape, 1) >= B - 8
        moved = jnp.where(far & (p > 0), 0.0, moved)
        a_ref[16:8 * last - 8, :] = moved - change
        c2 = columns(x2)
        nv = less(r1, t1, y)
        w = []
        for j in range(8):
            w.append(inv[j][j] * y[j])
            for i in range(j + 1, 8):
                w[j] = w[j] + inv[i][j] * y[i]
            w_ref[j:j + 1, :] = w[j][:1]
        nv1 = less(shift(x2), c2, w)
        rows = y[0]
        for j in range(1, 8):
            rows = jnp.where(sub == j, y[j], rows)
        v_ref[pl.ds(pl.multiple_of(p * 8, 8), 8), :] = rows
        return nv, nv1

    carry = d[0:8, :], d[8:16, :]
    for n in range(0, 16, STEP):
        carry = lax.fori_loop(n, n + STEP, functools.partial(panel, max(16 - n, 3)), carry)
    rows = lax.broadcasted_iota(jnp.int32, (B, B), 0)
    cols = lax.broadcasted_iota(jnp.int32, (B, B), 1)
    turned = [pltpu.roll(v_ref[8 * p:8 * p + 8, :], (8 * p + 8) % B, 1) for p in range(16)]
    return jnp.where(cols <= rows, jnp.concatenate(turned, axis=0), 0.0)


def after(k, inv, s_ref, hi_ref, lo_ref):
    k0, k1 = k * B, k * B + B
    if k1 < PIV:
        for j in range(k + 1, NB):
            s_ref[k0:k1, j * B:j * B + B] = jnp.zeros((B, B), jnp.float32)
        x = mm(split(s_ref[k1:, k0:k1]), split(inv))
        s_ref[k1:, k0:k1] = x
        h, l = split(x)
        hi_ref[k1:, :] = h
        lo_ref[k1:, :] = l
        for j in range(k + 1, NB):
            j0 = j * B
            s_ref[j0:, j0:j0 + B] = s_ref[j0:, j0:j0 + B] - mm(
                (hi_ref[j0:, :], lo_ref[j0:, :]), (hi_ref[j0:j0 + B, :], lo_ref[j0:j0 + B, :]))


def factor_steps(k_from, k_to, s_ref, dinv_ref, hi_ref, lo_ref, a_ref, w_ref, v_ref):
    rows = lax.broadcasted_iota(jnp.int32, (B, B), 0)
    cols = lax.broadcasted_iota(jnp.int32, (B, B), 1)

    def step(k, _):
        at = pl.ds(pl.multiple_of(k * B, B), B)
        d = s_ref[at, at]
        inv = diag_inverse(d, a_ref, w_ref, v_ref)
        dinv_ref[k] = inv
        own = lax.dot_general(d, inv, DN, precision=lax.Precision.HIGHEST, preferred_element_type=jnp.float32)
        s_ref[at, at] = jnp.where(cols <= rows, own, 0.0)
        for i in range(k_from, k_to):
            @pl.when(k == i)
            def _():
                after(i, inv, s_ref, hi_ref, lo_ref)
        return 0

    lax.fori_loop(k_from, k_to, step, 0)


def blocks_of(me):
    y, c = me // 2, me % 2
    near, far, across = (y + 3 - 2 * c) % NY, (y + 2) % NY, (y + 1 + 2 * c) % NY
    own = [2 * y + c, 2 * near + c, 2 * near + 1 - c, 2 * far + c]
    other = [2 * y + 1 - c, 2 * across + 1 - c, 2 * across + c, 2 * far + 1 - c]
    return own, other


def row_slice(block):
    return pl.ds(pl.multiple_of(block * B, B), B)


def chosen(values, n):
    return sum(jnp.where(n == i, v, 0) for i, v in enumerate(values))


def fetch(pairs, sems):
    copies = [pltpu.make_async_copy(src, dst, sems.at[n]) for n, (src, dst) in enumerate(pairs)]
    for copy in copies:
        copy.start()
    return copies


def first_kernel(*refs):
    pieces, (s_ref, dinv_ref), (g_ref, sems, *scratch) = refs[:8], refs[8:10], refs[10:]
    own, other = blocks_of(lax.axis_index("rows"))
    for copy in fetch([(r, g_ref.at[row_slice(n), :]) for r, n in zip(pieces, own + other)], sems):
        copy.wait()
    for i in range(NB):
        for j in range(i + 1):
            d = i - j
            if d < SLOTS:
                block = g_ref[i * B:i * B + B, d * B:d * B + B]
            else:
                t = NB - d
                block = g_ref[j * B:j * B + B, t * B:t * B + B].T
            s_ref[i * B:i * B + B, j * B:j * B + B] = block
    factor_steps(0, CUT, s_ref, dinv_ref, *scratch)


def second_kernel(s_in, dinv_in, s_ref, dinv_ref, *scratch):
    factor_steps(CUT, NB, s_ref, dinv_ref, *scratch)


def chol_scratch():
    return [
        pltpu.VMEM((PIV, B), jnp.bfloat16),
        pltpu.VMEM((PIV, B), jnp.bfloat16),
        pltpu.VMEM((B, B), jnp.float32),
        pltpu.VMEM((B, B), jnp.float32),
        pltpu.VMEM((B, B), jnp.float32),
    ]


VM = pl.BlockSpec(memory_space=pltpu.VMEM)
SM = pl.BlockSpec(memory_space=pltpu.SMEM)
ANY = pl.BlockSpec(memory_space=pl.ANY)
FACTOR = (
    jax.ShapeDtypeStruct((PIV, PIV), jnp.float32),
    jax.ShapeDtypeStruct((NB, B, B), jnp.float32),
)


def cost(flops):
    return pl.CostEstimate(flops=flops, bytes_accessed=4 * MIB, transcendentals=0)


def chol_first(pieces):
    return pl.pallas_call(
        first_kernel,
        in_specs=[ANY] * 8,
        out_shape=FACTOR,
        scratch_shapes=[pltpu.VMEM((PIV, SLOTS * B), jnp.float32), pltpu.SemaphoreType.DMA((8,))] + chol_scratch(),
        compiler_params=pltpu.CompilerParams(vmem_limit_bytes=18 * MIB),
        cost_estimate=cost(20 * 10**9),
        name="chol_first",
    )(*pieces)


def chol_second(s, dinv):
    return pl.pallas_call(
        second_kernel,
        in_specs=[VM] * 2,
        out_shape=FACTOR,
        scratch_shapes=chol_scratch(),
        input_output_aliases={0: 0, 1: 1},
        compiler_params=pltpu.CompilerParams(vmem_limit_bytes=18 * MIB),
        cost_estimate=cost(20 * 10**9),
        name="chol_second",
    )(s, dinv)


def solve_kernel(keep_ref, l_ref, dinv_ref, x0, x1, x2, x3, x_ref, fac_ref, c_ref, xh_ref, xl_ref, sems):
    copies = fetch([(r, c_ref.at[n * B:n * B + B, :]) for n, r in enumerate((x0, x1, x2, x3))], sems)
    keep = keep_ref[0] > 0
    fac_ref[0] = jnp.where(keep, l_ref[row_slice(lax.axis_index("rows")), :], 0.0)
    for copy in copies:
        copy.wait()

    def part(n, _):
        rows = pl.ds(pl.multiple_of(n * 2 * B, 2 * B), 2 * B)
        for k in range(NB):
            k0, k1 = k * B, k * B + B
            c = c_ref[rows, k0:k1]
            if k > 0:
                c = c - mm((xh_ref[:, :k0], xl_ref[:, :k0]), split(l_ref[k0:k1, :k0]))
            x = mm(split(c), split(dinv_ref[k]))
            x_ref[rows, k0:k1] = x
            xh_ref[:, k0:k1], xl_ref[:, k0:k1] = split(x)
        return 0

    lax.fori_loop(0, 2, part, 0)
    fac_ref[1] = jnp.where(keep, x_ref[:B, :], 0.0)


def solve(keep, s, dinv, pieces):
    return pl.pallas_call(
        solve_kernel,
        in_specs=[SM] + [VM] * 2 + [ANY] * 4,
        out_shape=(
            jax.ShapeDtypeStruct((PIV // 2, PIV), jnp.float32),
            jax.ShapeDtypeStruct((2, B, PIV), jnp.float32),
        ),
        scratch_shapes=[pltpu.VMEM((PIV // 2, PIV), jnp.float32)]
        + [pltpu.VMEM((2 * B, PIV), jnp.bfloat16)] * 2
        + [pltpu.SemaphoreType.DMA((4,))],
        compiler_params=pltpu.CompilerParams(vmem_limit_bytes=20 * MIB),
        cost_estimate=cost(3 * 10**9),
        name="solve",
    )(keep, s, dinv, *pieces)


def child_kernel(pos_ref, *refs):
    (x_in, xp_in, *pieces), (ec_ref, ep_ref, er_ref) = refs[:10], refs[10:13]
    x_ref, g_ref, u_ref, xh_ref, xl_ref, sems = refs[13:]
    me = lax.axis_index("rows")
    own, other = blocks_of(me)
    half = PIV // 2
    copies = fetch(
        [(r, g_ref.at[row_slice(n), :]) for r, n in zip(pieces, own + other)]
        + [(x_in, x_ref.at[:half, :]), (xp_in, x_ref.at[half:, :])],
        sems,
    )
    wanted = []
    for n in range(2):
        a = jnp.int32(-1)
        for b in range(NB):
            a = jnp.where(pos_ref[b] == me + n * NB, b, a)
        wanted.append((a >= 0, jnp.maximum(a, 0)))
    for copy in copies[:8]:
        copy.wait()
    for n, (_, a) in enumerate(wanted):
        for b in range(NB):
            t = (a + NB - b) % NB
            to = (slice(n * B, n * B + B), slice(b * B, b * B + B))

            @pl.when(t < SLOTS)
            def _():
                u_ref[to] = g_ref[row_slice(a), row_slice(t)]

            @pl.when(t >= SLOTS)
            def _():
                u_ref[to] = g_ref[b * B:b * B + B, row_slice(NB - t)].T
    for copy in copies[8:]:
        copy.wait()

    def place(n, _):
        block = chosen(own + other, n)
        h, l = split(x_ref[row_slice(n), :])
        xh_ref[row_slice(block), :] = h
        xl_ref[row_slice(block), :] = l
        return 0

    lax.fori_loop(0, NB, place, 0)
    some = tuple(jnp.concatenate([r[row_slice(a), :] for _, a in wanted], axis=0) for r in (xh_ref, xl_ref))

    def multiply(n, _):
        at = pl.ds(pl.multiple_of(n * 2 * B, 2 * B), 2 * B)
        u_ref[:, at] = u_ref[:, at] - mm(some, (xh_ref[at, :], xl_ref[at, :]))
        return 0

    lax.fori_loop(0, NB // 2, multiply, 0)
    for out_ref in (ec_ref, ep_ref, er_ref):
        out_ref[...] = jnp.zeros_like(out_ref)
    for b in range(NB):
        to = pos_ref[b]
        slot = (me + 2 * NB - to) % NB
        for held, hit, out_ref, at, n in (
            (wanted[0][0], (to < NB) & (slot < SLOTS), ec_ref, slot, 0),
            (wanted[1][0], to < NB, ep_ref, to % NB, 1),
            (wanted[1][0], to >= NB, er_ref, to % NB, 1),
        ):
            @pl.when(held & hit)
            def _():
                out_ref[:, row_slice(at)] = u_ref[n * B:n * B + B, b * B:b * B + B]


def child_update(positions, x, xp, rr):
    return pl.pallas_call(
        child_kernel,
        in_specs=[SM] + [ANY] * 10,
        out_shape=tuple(jax.ShapeDtypeStruct((B, n * B), jnp.float32) for n in (SLOTS, NB, NB)),
        scratch_shapes=[
            pltpu.VMEM((PIV, PIV), jnp.float32),
            pltpu.VMEM((PIV, SLOTS * B), jnp.float32),
            pltpu.VMEM((2 * B, PIV), jnp.float32),
            pltpu.VMEM((PIV, PIV), jnp.bfloat16),
            pltpu.VMEM((PIV, PIV), jnp.bfloat16),
            pltpu.SemaphoreType.DMA((10,)),
        ],
        compiler_params=pltpu.CompilerParams(vmem_limit_bytes=56 * MIB),
        cost_estimate=cost(3 * 10**9),
        name="child_update",
    )(positions, x, xp, *rr)


def product_kernel(x_in, xp_in, prod_ref, x_ref, sems):
    half = PIV // 2
    copies = fetch([(x_in, x_ref.at[:half, :]), (xp_in, x_ref.at[half:, :])], sems)
    own, other = blocks_of(lax.axis_index("rows"))
    for copy in copies:
        copy.wait()
    mine = split(x_ref[:B, :])

    def multiply(n, _):
        prod = mm(mine, split(x_ref[pl.ds(pl.multiple_of(n * 2 * B, 2 * B), 2 * B), :]))
        for i in range(2):
            prod_ref[:, row_slice(chosen(own + other, 2 * n + i))] = prod[:, i * B:i * B + B]
        return 0

    lax.fori_loop(0, NB // 2, multiply, 0)


def product(x, xp):
    return pl.pallas_call(
        product_kernel,
        in_specs=[ANY] * 2,
        out_shape=jax.ShapeDtypeStruct((B, PIV), jnp.float32),
        scratch_shapes=[pltpu.VMEM((PIV, PIV), jnp.float32), pltpu.SemaphoreType.DMA((2,))],
        compiler_params=pltpu.CompilerParams(vmem_limit_bytes=56 * MIB),
        cost_estimate=cost(10**9),
        name="product",
    )(x, xp)


def last_kernel(flags_ref, front_ref, sum_ref, got_ref, prod_ref, cb_ref):
    keep, same = flags_ref[0] > 0, flags_ref[1] > 0
    total = front_ref[...] + (sum_ref[...] + jnp.where(same, got_ref[...], 0.0))
    cb_ref[...] = jnp.where(keep, total - prod_ref[...], 0.0)


def parent_update(flags, front, sum_r, got, prod):
    whole = pl.BlockSpec((B, PIV), lambda g: (0, 0))
    return pl.pallas_call(
        last_kernel,
        grid=(1,),
        in_specs=[SM, pl.BlockSpec((None, None, None, B, PIV), lambda g: (0, 1, 0, 0, 1)), whole, whole, whole],
        out_specs=whole,
        out_shape=jax.ShapeDtypeStruct((B, PIV), jnp.float32),
        cost_estimate=pl.CostEstimate(flops=10**6, bytes_accessed=3 * MIB, transcendentals=0),
        name="parent_update",
    )(flags, front, sum_r, got, prod)


def pick(row_ref, out_ref):
    me = lax.axis_index("rows")
    for t in range(SLOTS):
        out_ref[:, t * B:t * B + B] = row_ref[:, row_slice((me + NB - t) % NB)]


def child_pieces_kernel(top_ref, low_ref, rest_ref, pp_ref, rp_ref, rr_ref):
    pick(top_ref, pp_ref)
    pick(rest_ref, rr_ref)
    rp_ref[...] = low_ref[...]


def parent_pieces_kernel(top_ref, pp_ref):
    pick(top_ref, pp_ref)


def pieces_of(kernel, front, quarters, widths):
    return pl.pallas_call(
        kernel,
        grid=(1,),
        in_specs=[pl.BlockSpec((None, None, None, B, PIV), lambda g, i=i, j=j: (0, i, 0, 0, j)) for i, j in quarters],
        out_specs=[pl.BlockSpec((B, n * B), lambda g: (0, 0)) for n in widths],
        out_shape=[jax.ShapeDtypeStruct((B, n * B), jnp.float32) for n in widths],
        cost_estimate=pl.CostEstimate(flops=0, bytes_accessed=MIB, transcendentals=0),
    )(*([front] * len(quarters)))


def to_next(x):
    return lax.ppermute(x, "rows", [(i, (i + 2 - 4 * (i % 2)) % NB) for i in range(NB)])


def to_partner(x):
    return lax.ppermute(x, "rows", [(i, i ^ 1) for i in range(NB)])


def from_right(x, shift):
    leaves = lax.axis_size("leaf")
    return lax.ppermute(x, "leaf", [(i + shift, i) for i in range(leaves - shift)])


def two_levels(child_front_entries, parent_fronts, parent_of, positions):
    leaf = lax.axis_index("leaf")
    padded = jnp.concatenate([jnp.full((1,), -1, jnp.int32), parent_of, jnp.full((2,), -1, jnp.int32)])
    near = lax.dynamic_slice(padded, (leaf,), (4,))
    head = (near[1:2] != near[0:1]).astype(jnp.int32)
    same1, same2 = near[1] == near[2], near[1] == near[3]
    every = jnp.ones((1,), jnp.int32)

    def add(x, got, same):
        return x + jnp.where(same, got, 0.0)

    def gather_pivots(x):
        across = to_partner(x)
        one = to_next(x)
        two = to_next(across)
        far = to_next(one)
        mine = [x, one, two, far]
        return mine + [across, to_partner(one), to_partner(two), to_partner(far)]

    pp, rp, rest = pieces_of(child_pieces_kernel, child_front_entries, ((0, 0), (1, 0), (1, 1)), (SLOTS, NB, SLOTS))
    pieces = gather_pivots(pp)
    across, across_r = to_partner(rp), to_partner(rest)
    one, two = to_next(rp), to_next(across)
    one_r, two_r = to_next(rest), to_next(across_r)
    s, dinv = chol_first(pieces)
    far, far_r = to_next(one), to_next(one_r)
    other_r = [across_r, to_partner(one_r), to_partner(two_r)]
    s, dinv = chol_second(s, dinv)
    other_r.append(to_partner(far_r))
    x, child_out = solve(every, s, dinv, [rp, one, two, far])
    rr = [rest, one_r, two_r, far_r] + other_r
    xp = to_partner(x)
    ext_c, ext_p, ext_r = child_update(positions[0], x, xp, rr)

    sum_c = add(ext_c, from_right(ext_c, 1), same1)
    got = from_right(sum_c, 2)
    sum_c = add(sum_c, got, same2)
    (pp,) = pieces_of(parent_pieces_kernel, parent_fronts, ((0, 0),), (SLOTS,))
    pieces = gather_pivots(pp + sum_c)
    got = from_right(ext_p, 1)
    sum_p = add(ext_p, got, same1)
    got = from_right(sum_p, 2)
    s, dinv = chol_first(pieces)
    rp = parent_fronts[0, 1, 0, :, :PIV] + add(sum_p, got, same2)
    across = to_partner(rp)
    one, two = to_next(rp), to_next(across)
    got = from_right(ext_r, 1)
    s, dinv = chol_second(s, dinv)
    far = to_next(one)
    sum_r = add(ext_r, got, same1)
    got = from_right(sum_r, 2)
    x, parent_out = solve(head, s, dinv, [rp, one, two, far])
    xp = to_partner(x)
    flags = jnp.concatenate([head, same2.astype(jnp.int32)[None]])
    prod = product(x, xp)
    block_out = parent_update(flags, parent_fronts, sum_r, got, prod)
    return (
        child_out[None, :, None],
        parent_out[None, :, None],
        block_out[None, None, None],
    )


def solution(mesh):
    placed = P("leaf", None, "rows", None, None)
    return jax.shard_map(
        two_levels,
        mesh=mesh,
        in_specs=(placed, placed, P(), P("leaf", None)),
        out_specs=(placed, placed, placed),
        check_vma=False,
    )
```

```python
import functools

import jax
import jax.numpy as jnp
from jax import lax
from jax.experimental import pallas as pl
from jax.experimental.pallas import tpu as pltpu
from jax.sharding import PartitionSpec as P


B = 128
PIV = 1024
NB = PIV // B
NY = NB // 2
SLOTS = 5
CUT = 5
KW = 16
STEP = 8
MIB = 2**20
DN = (((1,), (1,)), ((), ()))


def split(x):
    hi = x.astype(jnp.bfloat16)
    lo = (x - hi.astype(jnp.float32)).astype(jnp.bfloat16)
    return hi, lo


def dot(a, b):
    return lax.dot_general(a, b, DN, preferred_element_type=jnp.float32)


def mm(a, b):
    (ah, al), (bh, bl) = a, b
    return dot(ah, bh) + (dot(ah, bl) + dot(al, bh))


def wide(x):
    return jnp.broadcast_to(x, (8, B))


def sublane(x, i):
    return jnp.take_along_axis(x, jnp.full((8, B), i, jnp.int32), axis=0)


def columns(x):
    return [wide(x[:, j:j + 1]) for j in range(8)]


def less(x, c, w):
    t = [c[j] * w[j] for j in range(8)]
    return x - (((t[0] + t[1]) + (t[2] + t[3])) + ((t[4] + t[5]) + (t[6] + t[7])))


def diag_inverse(d, a_ref, w_ref, v_ref):
    sub = lax.broadcasted_iota(jnp.int32, (8, B), 0)
    lane = lax.broadcasted_iota(jnp.int32, (8, B), 1)
    done = lane >= B - 8
    unit = jnp.where(lane - (B - 8) == sub, 1.0, 0.0)
    a_ref[...] = pltpu.roll(d, 8, 1)
    w_ref[...] = jnp.zeros_like(w_ref)

    def shift(x):
        return jnp.where(done, 0.0, pltpu.roll(x, B - 8, 1))

    def panel(last, p, carry):
        v, v1 = carry
        zap = done & (p > 0)
        a2 = a_ref[16:24, :]
        c, t1, c2 = [], [], []
        c = columns(v)
        y = jnp.where(done, unit, pltpu.roll(v, B - 8, 1))
        for j in range(8):
            t1.append(wide(v1[:, j:j + 1]))
            c2.append(wide(a2[:, j:j + 1]))
        r1 = shift(v1)
        s = [[sublane(c[j], i) if i >= j else None for j in range(8)] for i in range(8)]
        y = [wide(y[j:j + 1, :]) for j in range(8)]
        w = [wide(w_ref[j:j + 1, :]) for j in range(8)]
        x2 = less(jnp.where(zap, 0.0, pltpu.roll(a2, B - 8, 1)), c2, w)
        r = [None] * 8
        inv = [[None] * 8 for _ in range(8)]
        for j in range(8):
            r[j] = lax.rsqrt(s[j][j])
            for i in range(j + 1, 8):
                s[i][j] = s[i][j] * r[j]
            for k in range(j + 1, 8):
                for i in range(k, 8):
                    s[i][k] = s[i][k] - s[i][j] * s[k][j]
            y[j] = y[j] * r[j]
            t1[j] = t1[j] * r[j]
            for i in range(j + 1, 8):
                y[i] = y[i] - s[i][j] * y[j]
                t1[i] = t1[i] - s[i][j] * t1[j]
            for k in range(j):
                inv[j][k] = inv[j][k] * r[j]
            inv[j][j] = r[j]
            for i in range(j + 1, 8):
                for k in range(j + 1):
                    m = s[i][j] * inv[j][k]
                    inv[i][k] = -m if inv[i][k] is None else inv[i][k] - m
        bulk = a_ref[24:8 * last, :]
        change = lax.dot_general(bulk[:, :KW], w_ref[:KW, :], (((1,), (0,)), ((), ())),
            precision=lax.Precision.HIGHEST, preferred_element_type=jnp.float32)
        moved = pltpu.roll(bulk, B - 8, 1)
        far = lax.broadcasted_iota(jnp.int32, bulk.shape, 1) >= B - 8
        moved = jnp.where(far & (p > 0), 0.0, moved)
        a_ref[16:8 * last - 8, :] = moved - change
        c2 = columns(x2)
        nv = less(r1, t1, y)
        w = []
        for j in range(8):
            w.append(inv[j][j] * y[j])
            for i in range(j + 1, 8):
                w[j] = w[j] + inv[i][j] * y[i]
            w_ref[j:j + 1, :] = w[j][:1]
        nv1 = less(shift(x2), c2, w)
        rows = y[0]
        for j in range(1, 8):
            rows = jnp.where(sub == j, y[j], rows)
        v_ref[pl.ds(pl.multiple_of(p * 8, 8), 8), :] = rows
        return nv, nv1

    carry = d[0:8, :], d[8:16, :]
    for n in range(0, 16, STEP):
        carry = lax.fori_loop(n, n + STEP, functools.partial(panel, max(16 - n, 3)), carry)
    rows = lax.broadcasted_iota(jnp.int32, (B, B), 0)
    cols = lax.broadcasted_iota(jnp.int32, (B, B), 1)
    turned = [pltpu.roll(v_ref[8 * p:8 * p + 8, :], (8 * p + 8) % B, 1) for p in range(16)]
    return jnp.where(cols <= rows, jnp.concatenate(turned, axis=0), 0.0)


def after(k, inv, s_ref, hi_ref, lo_ref):
    k0, k1 = k * B, k * B + B
    if k1 < PIV:
        for j in range(k + 1, NB):
            s_ref[k0:k1, j * B:j * B + B] = jnp.zeros((B, B), jnp.float32)
        x = mm(split(s_ref[k1:, k0:k1]), split(inv))
        s_ref[k1:, k0:k1] = x
        h, l = split(x)
        hi_ref[k1:, :] = h
        lo_ref[k1:, :] = l
        for j in range(k + 1, NB):
            j0 = j * B
            s_ref[j0:, j0:j0 + B] = s_ref[j0:, j0:j0 + B] - mm(
                (hi_ref[j0:, :], lo_ref[j0:, :]), (hi_ref[j0:j0 + B, :], lo_ref[j0:j0 + B, :]))


def factor_steps(k_from, k_to, s_ref, dinv_ref, hi_ref, lo_ref, a_ref, w_ref, v_ref):
    rows = lax.broadcasted_iota(jnp.int32, (B, B), 0)
    cols = lax.broadcasted_iota(jnp.int32, (B, B), 1)

    def step(k, _):
        at = pl.ds(pl.multiple_of(k * B, B), B)
        d = s_ref[at, at]
        inv = diag_inverse(d, a_ref, w_ref, v_ref)
        dinv_ref[k] = inv
        own = lax.dot_general(d, inv, DN, precision=lax.Precision.HIGHEST, preferred_element_type=jnp.float32)
        s_ref[at, at] = jnp.where(cols <= rows, own, 0.0)
        for i in range(k_from, k_to):
            @pl.when(k == i)
            def _():
                after(i, inv, s_ref, hi_ref, lo_ref)
        return 0

    lax.fori_loop(k_from, k_to, step, 0)


def blocks_of(me):
    y, c = me // 2, me % 2
    near, far, across = (y + 3 - 2 * c) % NY, (y + 2) % NY, (y + 1 + 2 * c) % NY
    own = [2 * y + c, 2 * near + c, 2 * near + 1 - c, 2 * far + c]
    other = [2 * y + 1 - c, 2 * across + 1 - c, 2 * across + c, 2 * far + 1 - c]
    return own, other


def row_slice(block):
    return pl.ds(pl.multiple_of(block * B, B), B)


def chosen(values, n):
    return sum(jnp.where(n == i, v, 0) for i, v in enumerate(values))


def fetch(pairs, sems):
    copies = [pltpu.make_async_copy(src, dst, sems.at[n]) for n, (src, dst) in enumerate(pairs)]
    for copy in copies:
        copy.start()
    return copies


def first_kernel(*refs):
    pieces, (s_ref, dinv_ref), (g_ref, sems, *scratch) = refs[:8], refs[8:10], refs[10:]
    own, other = blocks_of(lax.axis_index("rows"))
    for copy in fetch([(r, g_ref.at[row_slice(n), :]) for r, n in zip(pieces, own + other)], sems):
        copy.wait()
    for i in range(NB):
        for j in range(i + 1):
            d = i - j
            if d < SLOTS:
                block = g_ref[i * B:i * B + B, d * B:d * B + B]
            else:
                t = NB - d
                block = g_ref[j * B:j * B + B, t * B:t * B + B].T
            s_ref[i * B:i * B + B, j * B:j * B + B] = block
    factor_steps(0, CUT, s_ref, dinv_ref, *scratch)


def second_kernel(s_in, dinv_in, s_ref, dinv_ref, *scratch):
    factor_steps(CUT, NB, s_ref, dinv_ref, *scratch)


def chol_scratch():
    return [
        pltpu.VMEM((PIV, B), jnp.bfloat16),
        pltpu.VMEM((PIV, B), jnp.bfloat16),
        pltpu.VMEM((B, B), jnp.float32),
        pltpu.VMEM((B, B), jnp.float32),
        pltpu.VMEM((B, B), jnp.float32),
    ]


VM = pl.BlockSpec(memory_space=pltpu.VMEM)
SM = pl.BlockSpec(memory_space=pltpu.SMEM)
ANY = pl.BlockSpec(memory_space=pl.ANY)
FACTOR = (
    jax.ShapeDtypeStruct((PIV, PIV), jnp.float32),
    jax.ShapeDtypeStruct((NB, B, B), jnp.float32),
)


def cost(flops):
    return pl.CostEstimate(flops=flops, bytes_accessed=4 * MIB, transcendentals=0)


def chol_first(pieces):
    return pl.pallas_call(
        first_kernel,
        in_specs=[ANY] * 8,
        out_shape=FACTOR,
        scratch_shapes=[pltpu.VMEM((PIV, SLOTS * B), jnp.float32), pltpu.SemaphoreType.DMA((8,))] + chol_scratch(),
        compiler_params=pltpu.CompilerParams(vmem_limit_bytes=18 * MIB),
        cost_estimate=cost(20 * 10**9),
        name="chol_first",
    )(*pieces)


def chol_second(s, dinv):
    return pl.pallas_call(
        second_kernel,
        in_specs=[VM] * 2,
        out_shape=FACTOR,
        scratch_shapes=chol_scratch(),
        input_output_aliases={0: 0, 1: 1},
        compiler_params=pltpu.CompilerParams(vmem_limit_bytes=18 * MIB),
        cost_estimate=cost(20 * 10**9),
        name="chol_second",
    )(s, dinv)


def solve_kernel(keep_ref, l_ref, dinv_ref, x0, x1, x2, x3, x_ref, fac_ref, c_ref, xh_ref, xl_ref, sems):
    copies = fetch([(r.at[:, :PIV], c_ref.at[n * B:n * B + B, :]) for n, r in enumerate((x0, x1, x2, x3))], sems)
    keep = keep_ref[0] > 0
    fac_ref[0] = jnp.where(keep, l_ref[row_slice(lax.axis_index("rows")), :], 0.0)
    for copy in copies:
        copy.wait()

    def part(n, _):
        rows = pl.ds(pl.multiple_of(n * 2 * B, 2 * B), 2 * B)
        for k in range(0, NB, 2):
            k0, k1, k2 = k * B, k * B + B, k * B + 2 * B
            c = c_ref[rows, k0:k2]
            if k > 0:
                c = c - mm((xh_ref[:, :k0], xl_ref[:, :k0]), split(l_ref[k0:k2, :k0]))
            x = mm(split(c[:, :B]), split(dinv_ref[k]))
            x_ref[rows, k0:k1] = x
            halves = split(x)
            xh_ref[:, k0:k1], xl_ref[:, k0:k1] = halves
            c = c[:, B:] - mm(halves, split(l_ref[k1:k2, k0:k1]))
            x = mm(split(c), split(dinv_ref[k + 1]))
            x_ref[rows, k1:k2] = x
            xh_ref[:, k1:k2], xl_ref[:, k1:k2] = split(x)
        return 0

    lax.fori_loop(0, 2, part, 0)
    fac_ref[1] = jnp.where(keep, x_ref[:B, :], 0.0)


def solve(keep, s, dinv, pieces):
    return pl.pallas_call(
        solve_kernel,
        in_specs=[SM] + [VM] * 2 + [ANY] * 4,
        out_shape=(
            jax.ShapeDtypeStruct((PIV // 2, PIV), jnp.float32),
            jax.ShapeDtypeStruct((2, B, PIV), jnp.float32),
        ),
        scratch_shapes=[pltpu.VMEM((PIV // 2, PIV), jnp.float32)]
        + [pltpu.VMEM((2 * B, PIV), jnp.bfloat16)] * 2
        + [pltpu.SemaphoreType.DMA((4,))],
        compiler_params=pltpu.CompilerParams(vmem_limit_bytes=20 * MIB),
        cost_estimate=cost(3 * 10**9),
        name="solve",
    )(keep, s, dinv, *pieces)


def child_kernel(pos_ref, *refs):
    (x_in, xp_in, *pieces), (ec_ref, ep_ref, er_ref) = refs[:10], refs[10:13]
    x_ref, g_ref, u_ref, xh_ref, xl_ref, sems = refs[13:]
    me = lax.axis_index("rows")
    own, other = blocks_of(me)
    half = PIV // 2
    copies = fetch(
        [(r.at[:, PIV:], g_ref.at[row_slice(n), :]) for r, n in zip(pieces, own + other)]
        + [(x_in, x_ref.at[:half, :]), (xp_in, x_ref.at[half:, :])],
        sems,
    )
    wanted = []
    for n in range(2):
        a = jnp.int32(-1)
        for b in range(NB):
            a = jnp.where(pos_ref[b] == me + n * NB, b, a)
        wanted.append((a >= 0, jnp.maximum(a, 0)))
    for copy in copies[:8]:
        copy.wait()
    for n, (_, a) in enumerate(wanted):
        for b in range(NB):
            t = (a + NB - b) % NB
            to = (slice(n * B, n * B + B), slice(b * B, b * B + B))

            @pl.when(t < SLOTS)
            def _():
                u_ref[to] = g_ref[row_slice(a), row_slice(t)]

            @pl.when(t >= SLOTS)
            def _():
                u_ref[to] = g_ref[b * B:b * B + B, row_slice(NB - t)].T
    for copy in copies[8:]:
        copy.wait()

    def place(n, _):
        block = chosen(own + other, n)
        h, l = split(x_ref[row_slice(n), :])
        xh_ref[row_slice(block), :] = h
        xl_ref[row_slice(block), :] = l
        return 0

    lax.fori_loop(0, NB, place, 0)
    some = tuple(jnp.concatenate([r[row_slice(a), :] for _, a in wanted], axis=0) for r in (xh_ref, xl_ref))

    def multiply(n, _):
        at = pl.ds(pl.multiple_of(n * 2 * B, 2 * B), 2 * B)
        u_ref[:, at] = u_ref[:, at] - mm(some, (xh_ref[at, :], xl_ref[at, :]))
        return 0

    lax.fori_loop(0, NB // 2, multiply, 0)
    for out_ref in (ec_ref, ep_ref, er_ref):
        out_ref[...] = jnp.zeros_like(out_ref)
    for b in range(NB):
        to = pos_ref[b]
        slot = (me + 2 * NB - to) % NB
        for held, hit, out_ref, at, n in (
            (wanted[0][0], (to < NB) & (slot < SLOTS), ec_ref, slot, 0),
            (wanted[1][0], to < NB, ep_ref, to % NB, 1),
            (wanted[1][0], to >= NB, er_ref, to % NB, 1),
        ):
            @pl.when(held & hit)
            def _():
                out_ref[:, row_slice(at)] = u_ref[n * B:n * B + B, b * B:b * B + B]


def child_update(positions, x, xp, rr):
    return pl.pallas_call(
        child_kernel,
        in_specs=[SM] + [ANY] * 10,
        out_shape=tuple(jax.ShapeDtypeStruct((B, n * B), jnp.float32) for n in (SLOTS, NB, NB)),
        scratch_shapes=[
            pltpu.VMEM((PIV, PIV), jnp.float32),
            pltpu.VMEM((PIV, SLOTS * B), jnp.float32),
            pltpu.VMEM((2 * B, PIV), jnp.float32),
            pltpu.VMEM((PIV, PIV), jnp.bfloat16),
            pltpu.VMEM((PIV, PIV), jnp.bfloat16),
            pltpu.SemaphoreType.DMA((10,)),
        ],
        compiler_params=pltpu.CompilerParams(vmem_limit_bytes=56 * MIB),
        cost_estimate=cost(3 * 10**9),
        name="child_update",
    )(positions, x, xp, *rr)


def product_kernel(x_in, xp_in, prod_ref, x_ref, sems):
    half = PIV // 2
    copies = fetch([(x_in, x_ref.at[:half, :]), (xp_in, x_ref.at[half:, :])], sems)
    own, other = blocks_of(lax.axis_index("rows"))
    for copy in copies:
        copy.wait()
    mine = split(x_ref[:B, :])

    def multiply(n, _):
        prod = mm(mine, split(x_ref[pl.ds(pl.multiple_of(n * 2 * B, 2 * B), 2 * B), :]))
        for i in range(2):
            prod_ref[:, row_slice(chosen(own + other, 2 * n + i))] = prod[:, i * B:i * B + B]
        return 0

    lax.fori_loop(0, NB // 2, multiply, 0)


def product(x, xp):
    return pl.pallas_call(
        product_kernel,
        in_specs=[ANY] * 2,
        out_shape=jax.ShapeDtypeStruct((B, PIV), jnp.float32),
        scratch_shapes=[pltpu.VMEM((PIV, PIV), jnp.float32), pltpu.SemaphoreType.DMA((2,))],
        compiler_params=pltpu.CompilerParams(vmem_limit_bytes=56 * MIB),
        cost_estimate=cost(10**9),
        name="product",
    )(x, xp)


def last_kernel(flags_ref, front_ref, sum_ref, got_ref, prod_ref, cb_ref):
    keep, same = flags_ref[0] > 0, flags_ref[1] > 0
    total = front_ref[...] + (sum_ref[...] + jnp.where(same, got_ref[...], 0.0))
    cb_ref[...] = jnp.where(keep, total - prod_ref[...], 0.0)


def parent_update(flags, front, sum_r, got, prod):
    whole = pl.BlockSpec((B, PIV), lambda g: (0, 0))
    return pl.pallas_call(
        last_kernel,
        grid=(1,),
        in_specs=[SM, pl.BlockSpec((None, None, None, B, PIV), lambda g: (0, 1, 0, 0, 1)), whole, whole, whole],
        out_specs=whole,
        out_shape=jax.ShapeDtypeStruct((B, PIV), jnp.float32),
        cost_estimate=pl.CostEstimate(flops=10**6, bytes_accessed=3 * MIB, transcendentals=0),
        name="parent_update",
    )(flags, front, sum_r, got, prod)


def pick(row_ref, out_ref):
    me = lax.axis_index("rows")
    for t in range(SLOTS):
        out_ref[:, t * B:t * B + B] = row_ref[:, row_slice((me + NB - t) % NB)]


def child_pieces_kernel(top_ref, low_ref, rest_ref, pp_ref, low_out_ref):
    pick(top_ref, pp_ref)
    low_out_ref[:, :PIV] = low_ref[...]
    pick(rest_ref, low_out_ref.at[:, PIV:])


def parent_pieces_kernel(top_ref, pp_ref):
    pick(top_ref, pp_ref)


def pieces_of(kernel, front, quarters, widths):
    return pl.pallas_call(
        kernel,
        grid=(1,),
        in_specs=[pl.BlockSpec((None, None, None, B, PIV), lambda g, i=i, j=j: (0, i, 0, 0, j)) for i, j in quarters],
        out_specs=[pl.BlockSpec((B, n * B), lambda g: (0, 0)) for n in widths],
        out_shape=[jax.ShapeDtypeStruct((B, n * B), jnp.float32) for n in widths],
        cost_estimate=pl.CostEstimate(flops=0, bytes_accessed=MIB, transcendentals=0),
    )(*([front] * len(quarters)))


def to_next(x):
    return lax.ppermute(x, "rows", [(i, (i + 2 - 4 * (i % 2)) % NB) for i in range(NB)])


def to_partner(x):
    return lax.ppermute(x, "rows", [(i, i ^ 1) for i in range(NB)])


def from_right(x, shift):
    leaves = lax.axis_size("leaf")
    return lax.ppermute(x, "leaf", [(i + shift, i) for i in range(leaves - shift)])


def two_levels(child_front_entries, parent_fronts, parent_of, positions):
    leaf = lax.axis_index("leaf")
    padded = jnp.concatenate([jnp.full((1,), -1, jnp.int32), parent_of, jnp.full((2,), -1, jnp.int32)])
    near = lax.dynamic_slice(padded, (leaf,), (4,))
    head = (near[1:2] != near[0:1]).astype(jnp.int32)
    same1, same2 = near[1] == near[2], near[1] == near[3]
    every = jnp.ones((1,), jnp.int32)

    def add(x, got, same):
        return x + jnp.where(same, got, 0.0)

    def gather_pivots(x):
        across = to_partner(x)
        one = to_next(x)
        two = to_next(across)
        far = to_next(one)
        mine = [x, one, two, far]
        return mine + [across, to_partner(one), to_partner(two), to_partner(far)]

    pp, low = pieces_of(child_pieces_kernel, child_front_entries, ((0, 0), (1, 0), (1, 1)), (SLOTS, NB + SLOTS))
    pieces = gather_pivots(pp)
    across = to_partner(low)
    one, two = to_next(low), to_next(across)
    s, dinv = chol_first(pieces)
    far = to_next(one)
    others = [across, to_partner(one), to_partner(two)]
    s, dinv = chol_second(s, dinv)
    others.append(to_partner(far))
    x, child_out = solve(every, s, dinv, [low, one, two, far])
    rr = [low, one, two, far] + others
    xp = to_partner(x)
    ext_c, ext_p, ext_r = child_update(positions[0], x, xp, rr)

    sum_c = add(ext_c, from_right(ext_c, 1), same1)
    got = from_right(sum_c, 2)
    sum_c = add(sum_c, got, same2)
    (pp,) = pieces_of(parent_pieces_kernel, parent_fronts, ((0, 0),), (SLOTS,))
    pieces = gather_pivots(pp + sum_c)
    got = from_right(ext_p, 1)
    sum_p = add(ext_p, got, same1)
    got = from_right(sum_p, 2)
    s, dinv = chol_first(pieces)
    rp = parent_fronts[0, 1, 0, :, :PIV] + add(sum_p, got, same2)
    across = to_partner(rp)
    one, two = to_next(rp), to_next(across)
    got = from_right(ext_r, 1)
    s, dinv = chol_second(s, dinv)
    far = to_next(one)
    sum_r = add(ext_r, got, same1)
    got = from_right(sum_r, 2)
    x, parent_out = solve(head, s, dinv, [rp, one, two, far])
    xp = to_partner(x)
    flags = jnp.concatenate([head, same2.astype(jnp.int32)[None]])
    prod = product(x, xp)
    block_out = parent_update(flags, parent_fronts, sum_r, got, prod)
    return (
        child_out[None, :, None],
        parent_out[None, :, None],
        block_out[None, None, None],
    )


def solution(mesh):
    placed = P("leaf", None, "rows", None, None)
    return jax.shard_map(
        two_levels,
        mesh=mesh,
        in_specs=(placed, placed, P(), P("leaf", None)),
        out_specs=(placed, placed, placed),
        check_vma=False,
    )
```
